256 devices in a mesh: row: 8 (over y, core), col: 32 (over z, x).
Axes of the slice: x: 4, y: 4, z: 8, core: 2. Of those that a mesh axis runs over, the one named last changes fastest.
Arguments:
- observed: float32 [16384, 128], P(('row', 'col')), may hold values from -60 to 60
- lengths: int32 [16384], P(('row', 'col')), may hold values from 0 to 128
- features: float32 [16384, 32], P(('row', 'col')), may hold values from -6 to 6
- length_scale: float32 [32], replicated, may hold values from 2 to 5
- epoch_gain: float32 [128], replicated, may hold values from 0.5 to 2
Outputs:
- solution_field: float32 [16384, 128], P(('row', 'col'))
- residual: float32 [16384, 128], P(('row', 'col'))
The draws below stay inside these ranges and needn't reach their ends.
All inputs are finite; a program needn't handle non-finite values.
Results may differ from the reference program's by a relative error of at most 0.007.
Values may be sent and summed in bfloat16 or wider, within the bound.
No kernel may reach another device: no remote copies, remote signals or barrier semaphores. Data moves between devices by JAX's collectives and lax.ppermute only.
A program may use at most 64 MiB of HBM per device.

```python
import math
import jax
import jax.numpy as jnp
from jax import lax

E = 128
F = 32
ITERS = 2
N_TRIALS = 16384


def draw_observed(key, part):
    rows = jnp.arange(N_TRIALS).astype(jnp.float32)
    rise = 1.0 + 2.0 * rows / max(N_TRIALS - 1, 1)
    values = jnp.clip(jax.random.normal(key, (N_TRIALS, E), jnp.float32), -4.0, 4.0)
    return values * rise[:, None]


def touch_ends(drawn, stream_key, least, top_value):
    longest = drawn.shape.index(max(drawn.shape))
    spots = []
    for shift in (0, 1):
        where = [jax.random.randint(jax.random.fold_in(stream_key, axis), (), 0, length) for axis, length in enumerate(drawn.shape)]
        where[longest] = (where[longest] + shift) % drawn.shape[longest]
        spots.append(tuple(where))
    return drawn.at[spots[0]].set(least).at[spots[1]].set(top_value)


def levels(key, dims, cuts, low, top_value):
    def one(axis_at, blocks):
        steps = jax.random.uniform(jax.random.fold_in(jax.random.fold_in(key, 6), axis_at), (blocks,), jnp.float32, low / len(cuts), top_value / len(cuts))
        return jnp.repeat(jnp.exp(steps), dims[axis_at] // blocks).reshape((-1,) + (1,) * (len(dims) - axis_at - 1))

    gain = one(*cuts[0])
    for cut in cuts[1:]:
        gain = gain * one(*cut)
    return gain


def normal_values(key, shape, width, limit, cuts=(), kind=jnp.bfloat16):
    loudness = levels(key, shape, cuts, -0.22, 0.18) if cuts else 1.0
    result = jax.random.normal(key, shape, jnp.float32) * width * loudness
    return jnp.minimum(jnp.maximum(result, -limit), limit).astype(kind)


def setup_inputs(seed: int = 0) -> dict:
    seeds = jax.random.split(jax.random.key(seed), 6)
    observed = draw_observed(jax.random.fold_in(seeds[5], 71), 0)
    lengths = touch_ends(jax.random.randint(seeds[1], (N_TRIALS,), 0, E + 1), jax.random.fold_in(seeds[1], 1), 0, E).astype(jnp.int32)
    features = normal_values(seeds[2], (N_TRIALS, F), 1.0, 6.0, ((0, 256),), jnp.float32)
    length_scale = jnp.clip(jnp.exp(jax.random.uniform(seeds[3], (F,), jnp.float32, math.log(2.0), math.log(5.0))), 2.0, 5.0)
    epoch_gain = jnp.clip(jnp.exp(jax.random.uniform(seeds[4], (E,), jnp.float32, math.log(0.5), math.log(2.0))), 0.5, 2.0)
    return {"observed": observed, "lengths": lengths, "features": features, "length_scale": length_scale, "epoch_gain": epoch_gain}


noise_level = 0.3
epoch_offset = 16.0


def epoch_matrix(epoch_gain):
    steps = jnp.arange(E).astype(jnp.float32)
    base = epoch_offset / (steps[:, None] + steps[None, :] + epoch_offset)
    return base + jnp.diag(epoch_gain)


def kernel_block(left, left_sq, right, right_sq):
    cross = jnp.dot(left, right.T, precision=lax.Precision.HIGHEST, preferred_element_type=jnp.float32)
    dist = jnp.maximum(left_sq[:, None] + right_sq[None, :] - 2.0 * cross, 0.0)
    return jnp.exp(-0.5 * dist).astype(jnp.bfloat16)


def reference(observed, lengths, features, length_scale, epoch_gain):
    scaled = features / length_scale[None, :]
    sq = jnp.sum(scaled * scaled, axis=1)
    mask = (jnp.arange(E)[None, :] < lengths[:, None]).astype(jnp.float32)
    epoch_kernel = epoch_matrix(epoch_gain)
    block = min(512, N_TRIALS)
    count = N_TRIALS // block

    def operate(field):
        mixed = jnp.dot(mask * field, epoch_kernel, precision=lax.Precision.HIGHEST,
                        preferred_element_type=jnp.float32).astype(jnp.bfloat16)

        def one_block(index):
            start = (index * block).astype(jnp.int32)
            left = lax.dynamic_slice_in_dim(scaled, start, block, 0)
            left_sq = lax.dynamic_slice_in_dim(sq, start, block, 0)
            return jnp.dot(kernel_block(left, left_sq, scaled, sq), mixed, preferred_element_type=jnp.float32)

        product = lax.map(one_block, jnp.arange(count, dtype=jnp.int32)).reshape(N_TRIALS, E)
        return mask * product + noise_level * field

    solution_field = jnp.zeros_like(observed)
    residual = mask * observed
    direction = residual
    norm_now = jnp.sum(residual * residual)
    for step in range(ITERS):
        image = operate(direction)
        alpha = norm_now / jnp.sum(direction * image)
        solution_field = solution_field + alpha * direction
        residual = residual - alpha * image
        norm_next = jnp.sum(residual * residual)
        direction = residual + (norm_next / norm_now) * direction
        norm_now = norm_next
    return solution_field, residual
```

```python
import math

import jax
import jax.numpy as jnp
from jax import lax
from jax.experimental import pallas as pl
from jax.experimental.pallas import tpu as pltpu
from jax.sharding import Mesh
from jax.sharding import PartitionSpec as P

Y, C, Z, X = "y", "c", "z", "x"
ALL = (Y, C, Z, X)

noise_level = 0.3
epoch_offset = 16.0
bf16 = jnp.bfloat16
f32 = jnp.float32
HIGHEST = lax.Precision.HIGHEST
VMEM = pl.BlockSpec(memory_space=pltpu.VMEM)


def ahead(x, axis, k):
    n = lax.axis_size(axis)
    return lax.ppermute(x, axis, [((i + k) % n, i) for i in range(n)])


def around(x, axis):
    n = lax.axis_size(axis)
    blocks = [x] + [ahead(x, axis, k) for k in range(1, n)]
    start = (n - lax.axis_index(axis)) % n * x.shape[0]
    return lax.dynamic_slice_in_dim(jnp.concatenate(blocks + blocks), start, n * x.shape[0], 0)


def to_all(x, axes):
    copies = jnp.broadcast_to(x, (lax.axis_size(axes), *x.shape))
    return lax.all_to_all(copies, axes, split_axis=0, concat_axis=0, tiled=True)


def epoch_matrix(gain_row):
    n = gain_row.shape[-1]
    s = lax.broadcasted_iota(jnp.int32, (n, n), 0)
    t = lax.broadcasted_iota(jnp.int32, (n, n), 1)
    base = epoch_offset / ((s + t).astype(f32) + epoch_offset)
    return base + jnp.where(s == t, gain_row, 0.0)


def prepare(observed, lengths, features, length_scale, epoch_gain):
    own, width = observed.shape
    n = features.shape[1]
    copies = 8

    def body(obs_ref, len_ref, feat_ref, scale_ref, gain_ref, v_ref, mask_ref, ek_ref, out_ref, left_ref):
        lane = lax.broadcasted_iota(jnp.int32, (own, width), 1)
        mask = (lane < len_ref[...]).astype(f32)
        v = mask * obs_ref[...]
        ek = epoch_matrix(gain_ref[...])
        mask_ref[...] = mask
        v_ref[...] = v
        ek_ref[...] = ek
        w = jnp.dot(v, ek, precision=HIGHEST, preferred_element_type=f32).astype(bf16)
        scaled = feat_ref[...] * (math.sqrt(math.log2(math.e)) / scale_ref[...])
        hi = scaled.astype(bf16)
        hi32 = hi.astype(f32)
        lo = (scaled - hi32).astype(bf16)
        lo32 = lo.astype(f32)
        sq = jnp.sum(hi32 * (-0.5 * hi32 - lo32), axis=1, keepdims=True)
        sq0 = sq.astype(bf16).astype(f32)
        sq1 = (sq - sq0).astype(bf16).astype(f32)
        sq2 = sq - sq0 - sq1
        col = lax.broadcasted_iota(jnp.int32, (n, width), 1)
        row = lax.broadcasted_iota(jnp.int32, (n, width), 0)
        first, second, third = (col == row + k * n for k in range(3))

        def place(x, *where):
            spot = either(where).astype(bf16)
            return jnp.dot(x, spot, preferred_element_type=f32)

        def tail(x, at):
            for k, piece in enumerate((sq0, sq1, sq2)):
                x = jnp.where(lane == at + k, piece, x)
            return x

        ones = ((lane >= 3 * n) & (lane < 3 * n + 6)).astype(f32)
        left = tail(place(hi, first, second) + place(lo, third) + ones, 3 * n)
        right = tail(place(hi, first, third) + place(lo, second) + ones, 3 * n + 3)
        left_ref[...] = left.astype(bf16)
        right = right.astype(bf16)
        for k in range(copies):
            out_ref[k, :own, :] = w
            out_ref[k, own:, :] = right

    return pl.pallas_call(
        body,
        out_shape=(
            jax.ShapeDtypeStruct((own, width), f32),
            jax.ShapeDtypeStruct((own, width), f32),
            jax.ShapeDtypeStruct((width, width), f32),
            jax.ShapeDtypeStruct((copies, 2 * own, width), bf16),
            jax.ShapeDtypeStruct((own, width), bf16),
        ),
        in_specs=[VMEM] * 5,
        out_specs=(VMEM,) * 5,
        name="prepare",
    )(observed, lengths[:, None], features, length_scale[None, :], epoch_gain[None, :])


def either(conditions):
    out = conditions[0]
    for c in conditions[1:]:
        out = out | c
    return out


def finish(moments, v0, v1, v2):
    def body(m_ref, v0_ref, v1_ref, v2_ref, x_ref, r_ref):
        m = jnp.sum(jnp.sum(m_ref[...], axis=0), axis=1, keepdims=True)
        m0, m1, m2, m3 = (m[k : k + 1, :] for k in range(4))
        alpha = m0 / m1
        norm = m0 + alpha * (alpha * m2 - 2.0 * m1)
        keep = 1.0 + norm / m0
        curve = keep * (keep * m1 - 2.0 * alpha * m2) + alpha * alpha * m3
        again = norm / curve
        on0 = alpha + again * keep
        on1 = again * alpha
        v0, v1 = v0_ref[...], v1_ref[...]
        x_ref[...] = on0 * v0 - on1 * v1
        r_ref[...] = v0 - on0 * v1 + on1 * v2_ref[...]

    out = jax.ShapeDtypeStruct(v0.shape, f32)
    return pl.pallas_call(
        body,
        out_shape=(out, out),
        in_specs=[VMEM] * 4,
        out_specs=(VMEM,) * 2,
        name="finish",
    )(moments, v0, v1, v2)


def block_kernel(left, right):
    e = lax.dot_general(left, right, (((1,), (1,)), ((), ())), preferred_element_type=f32)
    return jnp.exp2(jnp.minimum(e, 0.0)).astype(bf16)


def per_device(observed, lengths, features, length_scale, epoch_gain):
    own, width = observed.shape
    v0, mask, ek, outgoing, left = prepare(observed, lengths, features, length_scale, epoch_gain)
    got = lax.all_to_all(outgoing, Z, split_axis=0, concat_axis=0, tiled=True)
    lefts = around(around(left, Y), X)
    here = got.reshape(got.shape[0], 2, own, width)
    there = ahead(here, C, 1)
    k_here = block_kernel(lefts, here[:, 1].reshape(-1, width))
    k_there = block_kernel(lefts, there[:, 1].reshape(-1, width))

    def product(w_here, w_there):
        part = jnp.dot(k_here, w_here, preferred_element_type=f32)
        part = part + jnp.dot(k_there, w_there, preferred_element_type=f32)
        part = part.reshape(-1, own, width)
        got = lax.all_to_all(part, (X, Y), split_axis=0, concat_axis=0, tiled=True)
        return jnp.sum(got, axis=0)

    p = product(here[:, 0].reshape(-1, width), there[:, 0].reshape(-1, width))
    v1 = mask * p + noise_level * v0
    w = jnp.dot(mask * v1, ek, precision=HIGHEST, preferred_element_type=f32).astype(bf16)
    w_here = to_all(w, Z).reshape(-1, width)
    p = product(w_here, ahead(w_here, C, 1))
    v2 = mask * p + noise_level * v1
    m = jnp.concatenate(
        [jnp.sum(a * b, axis=0, keepdims=True) for a, b in ((v0, v0), (v0, v1), (v1, v1), (v1, v2))]
    )
    m = jnp.sum(to_all(m, (Y, X)), axis=0)
    return finish(to_all(m, (Z, C)), v0, v1, v2)


def solution(mesh):
    torus = Mesh(mesh.devices.reshape(4, 2, 8, 4), ALL)
    in_specs = (P(ALL, None), P(ALL), P(ALL, None), P(), P())
    out_specs = (P(ALL, None), P(ALL, None))
    return jax.shard_map(
        per_device, mesh=torus, in_specs=in_specs, out_specs=out_specs, check_vma=False
    )
```

```python
import math

import jax
import jax.numpy as jnp
from jax import lax
from jax.experimental import pallas as pl
from jax.experimental.pallas import tpu as pltpu
from jax.sharding import Mesh
from jax.sharding import PartitionSpec as P

Y, C, Z, X = "y", "c", "z", "x"
ALL = (Y, C, Z, X)

noise_level = 0.3
epoch_offset = 16.0
bf16 = jnp.bfloat16
f32 = jnp.float32
HIGHEST = lax.Precision.HIGHEST
VMEM = pl.BlockSpec(memory_space=pltpu.VMEM)


def ahead(x, axis, k):
    n = lax.axis_size(axis)
    return lax.ppermute(x, axis, [((i + k) % n, i) for i in range(n)])


def around(x, axis):
    return [x] + [ahead(x, axis, k) for k in range(1, lax.axis_size(axis))]


def to_all(x, axes):
    copies = jnp.broadcast_to(x, (lax.axis_size(axes), *x.shape))
    return lax.all_to_all(copies, axes, split_axis=0, concat_axis=0, tiled=True)


def epoch_matrix(gain_row):
    n = gain_row.shape[-1]
    s = lax.broadcasted_iota(jnp.int32, (n, n), 0)
    t = lax.broadcasted_iota(jnp.int32, (n, n), 1)
    base = epoch_offset / ((s + t).astype(f32) + epoch_offset)
    return base + jnp.where(s == t, gain_row, 0.0)


def column(row):
    n = row.shape[-1]
    eye = lax.broadcasted_iota(jnp.int32, (n, n), 0) == lax.broadcasted_iota(jnp.int32, (n, n), 1)
    return jnp.sum(jnp.where(eye, row, 0.0), axis=1, keepdims=True)


def sides(features, length_scale, width):
    n, own = features.shape
    scaled = features * column(math.sqrt(math.log2(math.e)) / length_scale)
    hi = scaled.astype(bf16)
    lo = (scaled - hi.astype(f32)).astype(bf16)
    col = lax.broadcasted_iota(jnp.int32, (n, width), 1)
    row = lax.broadcasted_iota(jnp.int32, (n, width), 0)
    first, second, third = (col == row + k * n for k in range(3))
    lane = lax.broadcasted_iota(jnp.int32, (own, width), 1)

    def place(x, where):
        spot = jnp.where(where, 1.0, 0.0).astype(bf16)
        return lax.dot_general(x, spot, (((0,), (0,)), ((), ())), preferred_element_type=f32)

    left = place(hi, first | second) + place(lo, third)
    right = place(hi, first | third) + place(lo, second)
    sq = -0.5 * jnp.sum(left * right, axis=1, keepdims=True)
    sq0 = sq.astype(bf16).astype(f32)
    sq1 = (sq - sq0).astype(bf16).astype(f32)
    sq2 = sq - sq0 - sq1

    def tail(x, squares, ones):
        for k, piece in enumerate((sq0, sq1, sq2)):
            x = jnp.where(lane == squares + k, piece, x)
        return jnp.where((lane >= ones) & (lane < ones + 3), 1.0, x).astype(bf16)

    return tail(left, 3 * n, 3 * n + 3), tail(right, 3 * n + 3, 3 * n)


def prepare(observed, lengths, features, length_scale, epoch_gain, copies):
    own, width = observed.shape

    def body(obs_ref, len_ref, feat_ref, scale_ref, gain_ref, v_ref, mask_ref, ek_ref, out_ref):
        lane = lax.broadcasted_iota(jnp.int32, (own, width), 1).astype(f32)
        mask = (lane < column(len_ref[...].astype(f32))).astype(f32)
        v = mask * obs_ref[...]
        ek = epoch_matrix(gain_ref[...])
        mask_ref[...] = mask
        v_ref[...] = v
        ek_ref[...] = ek
        w = jnp.dot(v, ek, precision=HIGHEST, preferred_element_type=f32).astype(bf16)
        right = sides(feat_ref[...], scale_ref[...], width)[1]
        for k in range(copies):
            out_ref[k, :own, :] = w
            out_ref[k, own:, :] = right

    return pl.pallas_call(
        body,
        out_shape=(
            jax.ShapeDtypeStruct((own, width), f32),
            jax.ShapeDtypeStruct((own, width), f32),
            jax.ShapeDtypeStruct((width, width), f32),
            jax.ShapeDtypeStruct((copies, 2 * own, width), bf16),
        ),
        in_specs=[VMEM] * 5,
        out_specs=(VMEM,) * 4,
        name="prepare",
    )(observed, lengths, features, length_scale, epoch_gain)


def left_side(features, length_scale, width):
    def body(feat_ref, scale_ref, left_ref):
        left_ref[...] = sides(feat_ref[...], scale_ref[...], width)[0]

    return pl.pallas_call(
        body,
        out_shape=jax.ShapeDtypeStruct((features.shape[1], width), bf16),
        in_specs=[VMEM] * 2,
        out_specs=VMEM,
        name="left_side",
    )(features, length_scale)


def arrange(blocks, here):
    ny = len(blocks)
    rows, width = blocks[0].shape
    nx = 4
    own = rows // nx

    def body(here_ref, *refs):
        out_ref = refs[-1]
        for j in range(ny):
            for i in range(nx):
                slot = lax.rem(here_ref[0] + j, ny) * nx + lax.rem(here_ref[1] + i, nx)
                out_ref[slot] = refs[j][i * own : (i + 1) * own, :]

    return pl.pallas_call(
        body,
        out_shape=jax.ShapeDtypeStruct((ny * nx, own, width), bf16),
        in_specs=[pl.BlockSpec(memory_space=pltpu.SMEM)] + [VMEM] * ny,
        out_specs=VMEM,
        name="arrange",
    )(here, *blocks).reshape(-1, width)


def measure(got, mask, v0, v1):
    def body(got_ref, mask_ref, v0_ref, v1_ref, v2_ref, m_ref):
        v0, v1 = v0_ref[...], v1_ref[...]
        v2 = mask_ref[...] * jnp.sum(got_ref[...], axis=0) + noise_level * v1
        v2_ref[...] = v2
        lane = lax.broadcasted_iota(jnp.int32, m_ref.shape, 1)
        m = jnp.zeros(m_ref.shape, f32)
        for k, (a, b) in enumerate(((v0, v0), (v0, v1), (v1, v1), (v1, v2))):
            total = jnp.sum(jnp.sum(a * b, axis=0, keepdims=True), axis=1, keepdims=True)
            m = jnp.where(lane == k, total, m)
        m_ref[...] = m

    own, width = v0.shape
    return pl.pallas_call(
        body,
        out_shape=(jax.ShapeDtypeStruct((own, width), f32), jax.ShapeDtypeStruct((1, width), f32)),
        in_specs=[VMEM] * 4,
        out_specs=(VMEM,) * 2,
        name="measure",
    )(got, mask, v0, v1)


def finish(moments, v0, v1, v2):
    def body(m_ref, v0_ref, v1_ref, v2_ref, x_ref, r_ref):
        m = jnp.sum(m_ref[...], axis=0, keepdims=True)
        lane = lax.broadcasted_iota(jnp.int32, m.shape, 1)

        def moment(k):
            return jnp.sum(jnp.where(lane == k, m, 0.0), axis=1, keepdims=True)

        m0, m1, m2, m3 = (moment(k) for k in range(4))
        alpha = m0 / m1
        norm = m0 + alpha * (alpha * m2 - 2.0 * m1)
        keep = 1.0 + norm / m0
        curve = keep * (keep * m1 - 2.0 * alpha * m2) + alpha * alpha * m3
        again = norm / curve
        on0 = alpha + again * keep
        on1 = again * alpha
        v0, v1 = v0_ref[...], v1_ref[...]
        x_ref[...] = on0 * v0 - on1 * v1
        r_ref[...] = v0 - on0 * v1 + on1 * v2_ref[...]

    out = jax.ShapeDtypeStruct(v0.shape, f32)
    return pl.pallas_call(
        body,
        out_shape=(out, out),
        in_specs=[VMEM] * 4,
        out_specs=(VMEM,) * 2,
        name="finish",
    )(moments, v0, v1, v2)


def block_kernel(left, right):
    e = lax.dot_general(left, right, (((1,), (1,)), ((), ())), preferred_element_type=f32)
    return jnp.exp2(jnp.minimum(e, 0.0)).astype(bf16)


def per_device(observed, lengths, features, length_scale, epoch_gain):
    own, width = observed.shape
    features, length_scale = features.T, length_scale[None, :]
    v0, mask, ek, outgoing = prepare(
        observed, lengths[None, :], features, length_scale, epoch_gain[None, :], lax.axis_size(Z)
    )
    here = lax.all_to_all(outgoing, Z, split_axis=0, concat_axis=0, tiled=True)
    left = left_side(features, length_scale, width)
    line = jnp.concatenate(around(left, X))
    lefts = arrange(around(line, Y), jnp.stack([lax.axis_index(Y), lax.axis_index(X)]))
    there = ahead(here, C, 1)
    k_here = block_kernel(lefts, here[:, own:].reshape(-1, width))
    k_there = block_kernel(lefts, there[:, own:].reshape(-1, width))

    def product(w_here, w_there):
        part = jnp.dot(k_here, w_here, preferred_element_type=f32)
        part = part + jnp.dot(k_there, w_there, preferred_element_type=f32)
        return lax.all_to_all(
            part.reshape(-1, own, width), (Y, X), split_axis=0, concat_axis=0, tiled=True
        )

    got = product(here[:, :own].reshape(-1, width), there[:, :own].reshape(-1, width))
    v1 = mask * jnp.sum(got, axis=0) + noise_level * v0
    w = jnp.dot(mask * v1, ek, precision=HIGHEST, preferred_element_type=f32).astype(bf16)
    w_here = to_all(w, Z).reshape(-1, width)
    v2, m = measure(product(w_here, ahead(w_here, C, 1)), mask, v0, v1)
    m = to_all(m + ahead(m, C, 1), (Y, Z, X))
    return finish(m.reshape(-1, width), v0, v1, v2)


def solution(mesh):
    torus = Mesh(mesh.devices.reshape(4, 2, 8, 4), ALL)
    in_specs = (P(ALL, None), P(ALL), P(ALL, None), P(), P())
    out_specs = (P(ALL, None), P(ALL, None))
    return jax.shard_map(
        per_device, mesh=torus, in_specs=in_specs, out_specs=out_specs, check_vma=False
    )
```

```python
import math

import jax
import jax.numpy as jnp
from jax import lax
from jax.experimental import pallas as pl
from jax.experimental.pallas import tpu as pltpu
from jax.sharding import Mesh
from jax.sharding import PartitionSpec as P

Y, C, Z, X = "y", "c", "z", "x"
ALL = (Y, C, Z, X)

noise_level = 0.3
epoch_offset = 16.0
bf16 = jnp.bfloat16
f32 = jnp.float32
HIGHEST = lax.Precision.HIGHEST
VMEM = pl.BlockSpec(memory_space=pltpu.VMEM)
ANY = pl.BlockSpec(memory_space=pl.ANY)


def ahead(x, axis, k):
    n = lax.axis_size(axis)
    return lax.ppermute(x, axis, [((i + k) % n, i) for i in range(n)])


def around(x, axis):
    n = lax.axis_size(axis)
    blocks = [x] + [ahead(x, axis, k) for k in range(1, n)]
    start = (n - lax.axis_index(axis)) % n * x.shape[0]
    return lax.dynamic_slice_in_dim(jnp.concatenate(blocks + blocks), start, n * x.shape[0], 0)


def to_all(x, axes):
    copies = jnp.broadcast_to(x, (lax.axis_size(axes), *x.shape))
    return lax.all_to_all(copies, axes, split_axis=0, concat_axis=0, tiled=True)


def epoch_matrix(gain_row):
    n = gain_row.shape[-1]
    s = lax.broadcasted_iota(jnp.int32, (n, n), 0)
    t = lax.broadcasted_iota(jnp.int32, (n, n), 1)
    base = epoch_offset / ((s + t).astype(f32) + epoch_offset)
    return base + jnp.where(s == t, gain_row, 0.0)


def column(row):
    n = row.shape[-1]
    eye = lax.broadcasted_iota(jnp.int32, (n, n), 0) == lax.broadcasted_iota(jnp.int32, (n, n), 1)
    return jnp.sum(jnp.where(eye, row, 0.0), axis=1, keepdims=True)


def sides(features, length_scale, width):
    n, own = features.shape
    scaled = features * column(math.sqrt(math.log2(math.e)) / length_scale)
    hi = scaled.astype(bf16)
    lo = (scaled - hi.astype(f32)).astype(bf16)
    col = lax.broadcasted_iota(jnp.int32, (n, width), 1)
    row = lax.broadcasted_iota(jnp.int32, (n, width), 0)
    first, second, third = (col == row + k * n for k in range(3))
    lane = lax.broadcasted_iota(jnp.int32, (own, width), 1)

    def place(x, where):
        spot = jnp.where(where, 1.0, 0.0).astype(bf16)
        return lax.dot_general(x, spot, (((0,), (0,)), ((), ())), preferred_element_type=f32)

    left = place(hi, first | second) + place(lo, third)
    right = place(hi, first | third) + place(lo, second)
    sq = -0.5 * jnp.sum(left * right, axis=1, keepdims=True)
    sq0 = sq.astype(bf16).astype(f32)
    sq1 = (sq - sq0).astype(bf16).astype(f32)
    sq2 = sq - sq0 - sq1

    def tail(x, squares, ones):
        for k, piece in enumerate((sq0, sq1, sq2)):
            x = jnp.where(lane == squares + k, piece, x)
        return jnp.where((lane >= ones) & (lane < ones + 3), 1.0, x).astype(bf16)

    return tail(left, 3 * n, 3 * n + 3), tail(right, 3 * n + 3, 3 * n)


def seen(lengths, own, width):
    lane = lax.broadcasted_iota(jnp.int32, (own, width), 1).astype(f32)
    return (lane < column(lengths.astype(f32))).astype(f32)


def prepare(observed, lengths, features, length_scale, epoch_gain, left, copies):
    own, width = observed.shape

    def body(obs_ref, len_ref, feat_ref, scale_ref, gain_ref, _, v_ref, out_ref):
        v = seen(len_ref[...], own, width) * obs_ref[...]
        ek = epoch_matrix(gain_ref[...])
        v_ref[...] = v
        w = jnp.dot(v, ek, precision=HIGHEST, preferred_element_type=f32).astype(bf16)
        right = sides(feat_ref[...], scale_ref[...], width)[1]
        for k in range(copies):
            out_ref[k, :own, :] = w
            out_ref[k, own:, :] = right

    return pl.pallas_call(
        body,
        out_shape=(
            jax.ShapeDtypeStruct((own, width), f32),
            jax.ShapeDtypeStruct((copies, 2 * own, width), bf16),
        ),
        in_specs=[VMEM] * 5 + [ANY],
        out_specs=(VMEM,) * 2,
        name="prepare",
    )(observed, lengths, features, length_scale, epoch_gain, left)


def meanwhile(lengths, epoch_gain, v0, after):
    own, width = v0.shape

    def body(len_ref, gain_ref, v_ref, _, mask_ref, ek_ref, m_ref):
        mask_ref[...] = seen(len_ref[...], own, width)
        ek_ref[...] = epoch_matrix(gain_ref[...])
        v = v_ref[...]
        m_ref[...] = jnp.sum(v * v, axis=0, keepdims=True)

    return pl.pallas_call(
        body,
        out_shape=(
            jax.ShapeDtypeStruct((own, width), f32),
            jax.ShapeDtypeStruct((width, width), f32),
            jax.ShapeDtypeStruct((1, width), f32),
        ),
        in_specs=[VMEM] * 3 + [ANY],
        out_specs=(VMEM,) * 3,
        name="meanwhile",
    )(lengths, epoch_gain, v0, after)


def moments(m0, v0, v1, after):
    def body(m_ref, v0_ref, v1_ref, _, out_ref):
        v0, v1 = v0_ref[...], v1_ref[...]
        out_ref[0:1, :] = m_ref[...]
        out_ref[1:2, :] = jnp.sum(v0 * v1, axis=0, keepdims=True)
        out_ref[2:3, :] = jnp.sum(v1 * v1, axis=0, keepdims=True)

    return pl.pallas_call(
        body,
        out_shape=jax.ShapeDtypeStruct((3, v0.shape[1]), f32),
        in_specs=[VMEM] * 3 + [ANY],
        out_specs=VMEM,
        name="moments",
    )(m0, v0, v1, after)


def left_side(features, length_scale, width):
    def body(feat_ref, scale_ref, left_ref):
        left_ref[...] = sides(feat_ref[...], scale_ref[...], width)[0]

    return pl.pallas_call(
        body,
        out_shape=jax.ShapeDtypeStruct((features.shape[1], width), bf16),
        in_specs=[VMEM] * 2,
        out_specs=VMEM,
        name="left_side",
    )(features, length_scale)


def finish(moments, v0, v1, v2):
    def body(m_ref, v0_ref, v1_ref, v2_ref, x_ref, r_ref):
        m = jnp.sum(jnp.sum(m_ref[...], axis=0), axis=1, keepdims=True)
        m0, m1, m2, m3 = (m[k : k + 1, :] for k in range(4))
        alpha = m0 / m1
        norm = m0 + alpha * (alpha * m2 - 2.0 * m1)
        keep = 1.0 + norm / m0
        curve = keep * (keep * m1 - 2.0 * alpha * m2) + alpha * alpha * m3
        again = norm / curve
        on0 = alpha + again * keep
        on1 = again * alpha
        v0, v1 = v0_ref[...], v1_ref[...]
        x_ref[...] = on0 * v0 - on1 * v1
        r_ref[...] = v0 - on0 * v1 + on1 * v2_ref[...]

    out = jax.ShapeDtypeStruct(v0.shape, f32)
    return pl.pallas_call(
        body,
        out_shape=(out, out),
        in_specs=[VMEM] * 4,
        out_specs=(VMEM,) * 2,
        name="finish",
    )(moments, v0, v1, v2)


def block_kernel(left, right):
    e = lax.dot_general(left, right, (((1,), (1,)), ((), ())), preferred_element_type=f32)
    return jnp.exp2(jnp.minimum(e, 0.0)).astype(bf16)


def per_device(observed, lengths, features, length_scale, epoch_gain):
    own, width = observed.shape
    features, length_scale = features.T, length_scale[None, :]
    lengths, epoch_gain = lengths[None, :], epoch_gain[None, :]
    left = left_side(features, length_scale, width)
    line = around(left, X)
    v0, outgoing = prepare(
        observed, lengths, features, length_scale, epoch_gain, left, lax.axis_size(Z)
    )
    here = lax.all_to_all(outgoing, Z, split_axis=0, concat_axis=0, tiled=True)
    lefts = around(line.reshape(-1, own, width), Y).reshape(-1, width)
    there = ahead(here, C, 1)
    k_here = block_kernel(lefts, here[:, own:].reshape(-1, width))
    k_there = block_kernel(lefts, there[:, own:].reshape(-1, width))

    def product(w_here, w_there):
        part = jnp.dot(k_here, w_here, preferred_element_type=f32)
        part = part + jnp.dot(k_there, w_there, preferred_element_type=f32)
        got = lax.all_to_all(
            part.reshape(-1, own, width), (Y, X), split_axis=0, concat_axis=0, tiled=True
        )
        return jnp.sum(got, axis=0), part[:8]

    p, part = product(here[:, :own].reshape(-1, width), there[:, :own].reshape(-1, width))
    mask, ek, m = meanwhile(lengths, epoch_gain, v0, part)
    v1 = mask * p + noise_level * v0
    w = jnp.dot(mask * v1, ek, precision=HIGHEST, preferred_element_type=f32).astype(bf16)
    w_here = to_all(w, Z).reshape(-1, width)
    p, part = product(w_here, ahead(w_here, C, 1))
    m = moments(m, v0, v1, part)
    v2 = mask * p + noise_level * v1
    m = jnp.concatenate([m, jnp.sum(v1 * v2, axis=0, keepdims=True)])
    return finish(to_all(m + ahead(m, C, 1), (Y, Z, X)), v0, v1, v2)


def solution(mesh):
    torus = Mesh(mesh.devices.reshape(4, 2, 8, 4), ALL)
    in_specs = (P(ALL, None), P(ALL), P(ALL, None), P(), P())
    out_specs = (P(ALL, None), P(ALL, None))
    return jax.shard_map(
        per_device, mesh=torus, in_specs=in_specs, out_specs=out_specs, check_vma=False
    )
```

```python
import math

import jax
import jax.numpy as jnp
from jax import lax
from jax.experimental import pallas as pl
from jax.experimental.pallas import tpu as pltpu
from jax.sharding import Mesh
from jax.sharding import PartitionSpec as P

Y, C, Z, X = "y", "c", "z", "x"
ALL = (Y, C, Z, X)

noise_level = 0.3
epoch_offset = 16.0
bf16 = jnp.bfloat16
f32 = jnp.float32
f16 = jnp.float16
HIGHEST = lax.Precision.HIGHEST
VMEM = pl.BlockSpec(memory_space=pltpu.VMEM)
ANY = pl.BlockSpec(memory_space=pl.ANY)


def ahead(x, axis, k):
    n = lax.axis_size(axis)
    return lax.ppermute(x, axis, [((i + k) % n, i) for i in range(n)])


def around(x, axis):
    n = lax.axis_size(axis)
    blocks = [x] + [ahead(x, axis, k) for k in range(1, n)]
    start = (n - lax.axis_index(axis)) % n * x.shape[0]
    return lax.dynamic_slice_in_dim(jnp.concatenate(blocks + blocks), start, n * x.shape[0], 0)


def to_all(x, axes):
    copies = jnp.broadcast_to(x, (lax.axis_size(axes), *x.shape))
    return lax.all_to_all(copies, axes, split_axis=0, concat_axis=0, tiled=True)


def epoch_matrix(gain_row):
    n = gain_row.shape[-1]
    s = lax.broadcasted_iota(jnp.int32, (n, n), 0)
    t = lax.broadcasted_iota(jnp.int32, (n, n), 1)
    base = epoch_offset / ((s + t).astype(f32) + epoch_offset)
    return base + jnp.where(s == t, gain_row, 0.0)


def column(row):
    n = row.shape[-1]
    eye = lax.broadcasted_iota(jnp.int32, (n, n), 0) == lax.broadcasted_iota(jnp.int32, (n, n), 1)
    return jnp.sum(jnp.where(eye, row, 0.0), axis=1, keepdims=True)


def sides(features, length_scale, width):
    n, own = features.shape
    scaled = features * column(math.sqrt(math.log2(math.e)) / length_scale)
    hi = scaled.astype(bf16)
    lo = (scaled - hi.astype(f32)).astype(bf16)
    col = lax.broadcasted_iota(jnp.int32, (n, width), 1)
    row = lax.broadcasted_iota(jnp.int32, (n, width), 0)
    first, second, third = (col == row + k * n for k in range(3))
    lane = lax.broadcasted_iota(jnp.int32, (own, width), 1)

    def place(x, where):
        spot = jnp.where(where, 1.0, 0.0).astype(bf16)
        return lax.dot_general(x, spot, (((0,), (0,)), ((), ())), preferred_element_type=f32)

    left = place(hi, first | second) + place(lo, third)
    right = place(hi, first | third) + place(lo, second)
    sq = -0.5 * jnp.sum(left * right, axis=1, keepdims=True)
    sq0 = sq.astype(bf16).astype(f32)
    sq1 = (sq - sq0).astype(bf16).astype(f32)
    sq2 = sq - sq0 - sq1

    def tail(x, squares, ones):
        for k, piece in enumerate((sq0, sq1, sq2)):
            x = jnp.where(lane == squares + k, piece, x)
        return jnp.where((lane >= ones) & (lane < ones + 3), 1.0, x).astype(bf16)

    return tail(left, 3 * n, 3 * n + 3), tail(right, 3 * n + 3, 3 * n)


def seen(lengths, own, width):
    lane = lax.broadcasted_iota(jnp.int32, (own, width), 1).astype(f32)
    return (lane < column(lengths.astype(f32))).astype(f32)


def prepare(observed, lengths, features, length_scale, epoch_gain, left, copies):
    own, width = observed.shape

    def body(obs_ref, len_ref, feat_ref, scale_ref, gain_ref, _, v_ref, mask_ref, ek_ref, out_ref):
        lane = lax.broadcasted_iota(jnp.int32, (own, width), 1).astype(f32)
        mask = (lane < column(len_ref[...].astype(f32))).astype(f32)
        v = mask * obs_ref[...]
        ek = epoch_matrix(gain_ref[...])
        mask_ref[...] = mask
        v_ref[...] = v
        ek_ref[...] = ek
        w = jnp.dot(v, ek, precision=HIGHEST, preferred_element_type=f32).astype(bf16)
        right = sides(feat_ref[...], scale_ref[...], width)[1]
        for k in range(copies):
            out_ref[k, :own, :] = w
            out_ref[k, own:, :] = right

    return pl.pallas_call(
        body,
        out_shape=(
            jax.ShapeDtypeStruct((own, width), f32),
            jax.ShapeDtypeStruct((own, width), f32),
            jax.ShapeDtypeStruct((width, width), f32),
            jax.ShapeDtypeStruct((copies, 2 * own, width), bf16),
        ),
        in_specs=[VMEM] * 5 + [ANY],
        out_specs=(VMEM,) * 4,
        name="prepare",
    )(observed, lengths, features, length_scale, epoch_gain, left)


def left_side(features, length_scale, width):
    def body(feat_ref, scale_ref, left_ref):
        left_ref[...] = sides(feat_ref[...], scale_ref[...], width)[0]

    return pl.pallas_call(
        body,
        out_shape=jax.ShapeDtypeStruct((features.shape[1], width), bf16),
        in_specs=[VMEM] * 2,
        out_specs=VMEM,
        name="left_side",
    )(features, length_scale)


def measure(v0, v1, v2):
    def body(v0_ref, v1_ref, v2_ref, m_ref):
        v0, v1, v2 = v0_ref[...], v1_ref[...], v2_ref[...]
        lane = lax.broadcasted_iota(jnp.int32, m_ref.shape, 1)
        m = jnp.zeros(m_ref.shape, f32)
        for k, (a, b) in enumerate(((v0, v0), (v0, v1), (v1, v1), (v1, v2))):
            total = jnp.sum(jnp.sum(a * b, axis=0, keepdims=True), axis=1, keepdims=True)
            m = jnp.where(lane == k, total, m)
        m_ref[...] = m

    return pl.pallas_call(
        body,
        out_shape=jax.ShapeDtypeStruct((1, v0.shape[1]), f32),
        in_specs=[VMEM] * 3,
        out_specs=VMEM,
        name="measure",
    )(v0, v1, v2)


def finish(moments, v0, v1, v2):
    def body(m_ref, v0_ref, v1_ref, v2_ref, x_ref, r_ref):
        m = jnp.sum(m_ref[...], axis=0, keepdims=True)
        lane = lax.broadcasted_iota(jnp.int32, m.shape, 1)

        def moment(k):
            return jnp.sum(jnp.where(lane == k, m, 0.0), axis=1, keepdims=True)

        m0, m1, m2, m3 = (moment(k) for k in range(4))
        alpha = m0 / m1
        norm = m0 + alpha * (alpha * m2 - 2.0 * m1)
        keep = 1.0 + norm / m0
        curve = keep * (keep * m1 - 2.0 * alpha * m2) + alpha * alpha * m3
        again = norm / curve
        on0 = alpha + again * keep
        on1 = again * alpha
        v0, v1 = v0_ref[...], v1_ref[...]
        x_ref[...] = on0 * v0 - on1 * v1
        r_ref[...] = v0 - on0 * v1 + on1 * v2_ref[...]

    out = jax.ShapeDtypeStruct(v0.shape, f32)
    return pl.pallas_call(
        body,
        out_shape=(out, out),
        in_specs=[VMEM] * 4,
        out_specs=(VMEM,) * 2,
        name="finish",
    )(moments, v0, v1, v2)


def block_kernel(left, right):
    e = lax.dot_general(left, right, (((1,), (1,)), ((), ())), preferred_element_type=f32)
    return jnp.exp2(jnp.minimum(e, 0.0)).astype(bf16)


def per_device(observed, lengths, features, length_scale, epoch_gain):
    own, width = observed.shape
    features, length_scale = features.T, length_scale[None, :]
    lengths, epoch_gain = lengths[None, :], epoch_gain[None, :]
    left = left_side(features, length_scale, width)
    line = around(left, X)
    v0, mask, ek, outgoing = prepare(
        observed, lengths, features, length_scale, epoch_gain, left, lax.axis_size(Z)
    )
    here = lax.all_to_all(outgoing, Z, split_axis=0, concat_axis=0, tiled=True)
    lefts = around(line.reshape(-1, own, width), Y).reshape(-1, width)
    there = ahead(here, C, 1)
    k_here = block_kernel(lefts, here[:, own:].reshape(-1, width))
    k_there = block_kernel(lefts, there[:, own:].reshape(-1, width))

    def product(w_here, w_there):
        part = jnp.dot(k_here, w_here, preferred_element_type=f32)
        part = part + jnp.dot(k_there, w_there, preferred_element_type=f32)
        top = jnp.maximum(*(jnp.max(jnp.abs(w.astype(f32)), axis=0) for w in (w_here, w_there)))
        power = jnp.ceil(jnp.log2(jnp.maximum(top, 1e-30) * (2 * w_here.shape[0])))
        part = (part * jnp.exp2(15.0 - power)).astype(f16).reshape(-1, own, width)
        tail = jnp.broadcast_to(power.astype(f16), (part.shape[0], 16, width))
        got = lax.all_to_all(
            jnp.concatenate([part, tail], axis=1), (Y, X), split_axis=0, concat_axis=0, tiled=True
        )
        scale = jnp.exp2(got[:, own : own + 1].astype(f32) - 15.0)
        return jnp.sum(got[:, :own].astype(f32) * scale, axis=0)

    p = product(here[:, :own].reshape(-1, width), there[:, :own].reshape(-1, width))
    v1 = mask * p + noise_level * v0
    w = jnp.dot(mask * v1, ek, precision=HIGHEST, preferred_element_type=f32).astype(bf16)
    w_here = to_all(w, Z).reshape(-1, width)
    p = product(w_here, ahead(w_here, C, 1))
    v2 = mask * p + noise_level * v1
    m = measure(v0, v1, v2)
    m = to_all(m + ahead(m, C, 1), (Y, Z, X)).reshape(-1, width)
    return finish(m, v0, v1, v2)


def solution(mesh):
    torus = Mesh(mesh.devices.reshape(4, 2, 8, 4), ALL)
    in_specs = (P(ALL, None), P(ALL), P(ALL, None), P(), P())
    out_specs = (P(ALL, None), P(ALL, None))
    return jax.shard_map(
        per_device, mesh=torus, in_specs=in_specs, out_specs=out_specs, check_vma=False
    )
```

```python
import math

import jax
import jax.numpy as jnp
from jax import lax
from jax.experimental import pallas as pl
from jax.experimental.pallas import tpu as pltpu
from jax.sharding import Mesh
from jax.sharding import PartitionSpec as P

Y, C, Z, X = "y", "c", "z", "x"
ALL = (Y, C, Z, X)

noise_level = 0.3
epoch_offset = 16.0
bf16 = jnp.bfloat16
f32 = jnp.float32
f16 = jnp.float16
HIGHEST = lax.Precision.HIGHEST
VMEM = pl.BlockSpec(memory_space=pltpu.VMEM)
ANY = pl.BlockSpec(memory_space=pl.ANY)


def ahead(x, axis, k):
    n = lax.axis_size(axis)
    return lax.ppermute(x, axis, [((i + k) % n, i) for i in range(n)])


def around(x, axis, base):
    n, me = lax.axis_size(axis), lax.axis_index(axis)
    for k in range(n):
        block = ahead(x, axis, k) if k else x
        base = lax.dynamic_update_slice_in_dim(base, block, (me + k) % n * x.shape[0], 0)
    return base


def to_all(x, axes):
    copies = jnp.broadcast_to(x, (lax.axis_size(axes), *x.shape))
    return lax.all_to_all(copies, axes, split_axis=0, concat_axis=0, tiled=True)


def epoch_matrix(gain_row):
    n = gain_row.shape[-1]
    s = lax.broadcasted_iota(jnp.int32, (n, n), 0)
    t = lax.broadcasted_iota(jnp.int32, (n, n), 1)
    base = epoch_offset / ((s + t).astype(f32) + epoch_offset)
    return base + jnp.where(s == t, gain_row, 0.0)


def column(row):
    n = row.shape[-1]
    eye = lax.broadcasted_iota(jnp.int32, (n, n), 0) == lax.broadcasted_iota(jnp.int32, (n, n), 1)
    return jnp.sum(jnp.where(eye, row, 0.0), axis=1, keepdims=True)


def sides(features, length_scale, width):
    n, own = features.shape
    scaled = features * column(math.sqrt(math.log2(math.e)) / length_scale)
    hi = scaled.astype(bf16)
    lo = (scaled - hi.astype(f32)).astype(bf16)
    col = lax.broadcasted_iota(jnp.int32, (n, width), 1)
    row = lax.broadcasted_iota(jnp.int32, (n, width), 0)
    first, second, third = (col == row + k * n for k in range(3))
    lane = lax.broadcasted_iota(jnp.int32, (own, width), 1)

    def place(x, where):
        spot = jnp.where(where, 1.0, 0.0).astype(bf16)
        return lax.dot_general(x, spot, (((0,), (0,)), ((), ())), preferred_element_type=f32)

    left = place(hi, first | second) + place(lo, third)
    right = place(hi, first | third) + place(lo, second)
    sq = -0.5 * jnp.sum(left * right, axis=1, keepdims=True)
    sq0 = sq.astype(bf16).astype(f32)
    sq1 = (sq - sq0).astype(bf16).astype(f32)
    sq2 = sq - sq0 - sq1

    def tail(x, squares, ones):
        for k, piece in enumerate((sq0, sq1, sq2)):
            x = jnp.where(lane == squares + k, piece, x)
        return jnp.where((lane >= ones) & (lane < ones + 3), 1.0, x).astype(bf16)

    return tail(left, 3 * n, 3 * n + 3), tail(right, 3 * n + 3, 3 * n)


def seen(lengths, own, width):
    lane = lax.broadcasted_iota(jnp.int32, (own, width), 1).astype(f32)
    return (lane < column(lengths.astype(f32))).astype(f32)


def prepare(observed, lengths, features, length_scale, epoch_gain):
    own, width = observed.shape

    def body(obs_ref, len_ref, feat_ref, scale_ref, gain_ref, v_ref, mask_ref, ek_ref, out_ref, left_ref):
        left, right = sides(feat_ref[...], scale_ref[...], width)
        left_ref[...] = left
        lane = lax.broadcasted_iota(jnp.int32, (own, width), 1).astype(f32)
        mask = (lane < column(len_ref[...].astype(f32))).astype(f32)
        v = mask * obs_ref[...]
        ek = epoch_matrix(gain_ref[...])
        mask_ref[...] = mask
        v_ref[...] = v
        ek_ref[...] = ek
        w = jnp.dot(v, ek, precision=HIGHEST, preferred_element_type=f32)
        out_ref[:own, :] = w.astype(bf16)
        out_ref[own:, :] = right

    return pl.pallas_call(
        body,
        out_shape=(
            jax.ShapeDtypeStruct((own, width), f32),
            jax.ShapeDtypeStruct((own, width), f32),
            jax.ShapeDtypeStruct((width, width), f32),
            jax.ShapeDtypeStruct((2 * own, width), bf16),
            jax.ShapeDtypeStruct((own, width), bf16),
        ),
        in_specs=[VMEM] * 5,
        out_specs=(VMEM,) * 5,
        name="prepare",
    )(observed, lengths, features, length_scale, epoch_gain)


def measure(p, mask, v0, v1):
    def body(p_ref, mask_ref, v0_ref, v1_ref, v2_ref, m_ref):
        v0, v1 = v0_ref[...], v1_ref[...]
        v2 = mask_ref[...] * p_ref[...] + noise_level * v1
        v2_ref[...] = v2
        lane = lax.broadcasted_iota(jnp.int32, m_ref.shape, 1)
        m = jnp.zeros(m_ref.shape, f32)
        for k, (a, b) in enumerate(((v0, v0), (v0, v1), (v1, v1), (v1, v2))):
            total = jnp.sum(jnp.sum(a * b, axis=0, keepdims=True), axis=1, keepdims=True)
            m = jnp.where(lane == k, total, m)
        m_ref[...] = m

    own, width = v0.shape
    return pl.pallas_call(
        body,
        out_shape=(jax.ShapeDtypeStruct((own, width), f32), jax.ShapeDtypeStruct((1, width), f32)),
        in_specs=[VMEM] * 4,
        out_specs=(VMEM,) * 2,
        name="measure",
    )(p, mask, v0, v1)


def finish(moments, v0, v1, v2):
    n = len(moments)

    def body(*refs):
        v0_ref, v1_ref, v2_ref, x_ref, r_ref = refs[n:]
        m = sum(ref[...] for ref in refs[1:n]) + refs[0][...]
        lane = lax.broadcasted_iota(jnp.int32, m.shape, 1)

        def moment(k):
            return jnp.sum(jnp.where(lane == k, m, 0.0), axis=1, keepdims=True)

        m0, m1, m2, m3 = (moment(k) for k in range(4))
        alpha = m0 / m1
        norm = m0 + alpha * (alpha * m2 - 2.0 * m1)
        keep = 1.0 + norm / m0
        curve = keep * (keep * m1 - 2.0 * alpha * m2) + alpha * alpha * m3
        again = norm / curve
        on0 = alpha + again * keep
        on1 = again * alpha
        v0, v1 = v0_ref[...], v1_ref[...]
        x_ref[...] = on0 * v0 - on1 * v1
        r_ref[...] = v0 - on0 * v1 + on1 * v2_ref[...]

    out = jax.ShapeDtypeStruct(v0.shape, f32)
    return pl.pallas_call(
        body,
        out_shape=(out, out),
        in_specs=[VMEM] * (n + 3),
        out_specs=(VMEM,) * 2,
        name="finish",
    )(*moments, v0, v1, v2)


def block_kernel(left, right):
    e = lax.dot_general(left, right, (((1,), (1,)), ((), ())), preferred_element_type=f32)
    return jnp.exp2(jnp.minimum(e, 0.0)).astype(bf16)


def per_device(observed, lengths, features, length_scale, epoch_gain):
    own, width = observed.shape
    features, length_scale = features.T, length_scale[None, :]
    lengths, epoch_gain = lengths[None, :], epoch_gain[None, :]
    v0, mask, ek, outgoing, left = prepare(observed, lengths, features, length_scale, epoch_gain)
    here = to_all(outgoing, Z)
    line = around(left, X, jnp.zeros((lax.axis_size(X) * own, width), bf16))
    there = ahead(here, C, 1)
    lefts = around(line, Y, here.reshape(-1, width))
    k_here = block_kernel(lefts, here[:, own:].reshape(-1, width))
    k_there = block_kernel(lefts, there[:, own:].reshape(-1, width))

    def product(w_here, w_there):
        part = jnp.dot(k_here, w_here, preferred_element_type=f32)
        part = part + jnp.dot(k_there, w_there, preferred_element_type=f32)
        top = jnp.maximum(*(jnp.max(jnp.abs(w.astype(f32)), axis=0) for w in (w_here, w_there)))
        power = jnp.ceil(jnp.log2(jnp.maximum(top, 1e-30) * (2 * w_here.shape[0])))
        part = (part * jnp.exp2(15.0 - power)).astype(f16).reshape(-1, own, width)
        tail = jnp.broadcast_to(power.astype(f16), (part.shape[0], 8, width))
        got = lax.all_to_all(
            jnp.concatenate([part, tail], axis=1), (Y, X), split_axis=0, concat_axis=0, tiled=True
        )
        scale = jnp.exp2(got[:, own : own + 1].astype(f32) - 15.0)
        return jnp.sum(got[:, :own].astype(f32) * scale, axis=0)

    p = product(here[:, :own].reshape(-1, width), there[:, :own].reshape(-1, width))
    v1 = mask * p + noise_level * v0
    w = jnp.dot(mask * v1, ek, precision=HIGHEST, preferred_element_type=f32).astype(bf16)
    w_here = to_all(w, Z).reshape(-1, width)
    p = product(w_here, ahead(w_here, C, 1))
    v2, m = measure(p, mask, v0, v1)
    m = jnp.sum(to_all(m, (C, Z, X)), axis=0)
    return finish([m] + [ahead(m, Y, k) for k in range(1, lax.axis_size(Y))], v0, v1, v2)


def solution(mesh):
    torus = Mesh(mesh.devices.reshape(4, 2, 8, 4), ALL)
    in_specs = (P(ALL, None), P(ALL), P(ALL, None), P(), P())
    out_specs = (P(ALL, None), P(ALL, None))
    return jax.shard_map(
        per_device, mesh=torus, in_specs=in_specs, out_specs=out_specs, check_vma=False
    )
```

```python
import math

import jax
import jax.numpy as jnp
from jax import lax
from jax.experimental import pallas as pl
from jax.experimental.pallas import tpu as pltpu
from jax.sharding import Mesh
from jax.sharding import PartitionSpec as P

Y, C, Z, X = "y", "c", "z", "x"
ALL = (Y, C, Z, X)

noise_level = 0.3
epoch_offset = 16.0
bf16 = jnp.bfloat16
f32 = jnp.float32
f16 = jnp.float16
HIGHEST = lax.Precision.HIGHEST
VMEM = pl.BlockSpec(memory_space=pltpu.VMEM)
ANY = pl.BlockSpec(memory_space=pl.ANY)


def ahead(x, axis, k):
    n = lax.axis_size(axis)
    return lax.ppermute(x, axis, [((i + k) % n, i) for i in range(n)])


def around(x, axis, base):
    n, me = lax.axis_size(axis), lax.axis_index(axis)
    for k in range(n):
        block = ahead(x, axis, k) if k else x
        base = lax.dynamic_update_slice_in_dim(base, block, (me + k) % n * x.shape[0], 0)
    return base


def to_all(x, axes):
    copies = jnp.broadcast_to(x, (lax.axis_size(axes), *x.shape))
    return lax.all_to_all(copies, axes, split_axis=0, concat_axis=0, tiled=True)


def epoch_matrix(gain_row):
    n = gain_row.shape[-1]
    s = lax.broadcasted_iota(jnp.int32, (n, n), 0)
    t = lax.broadcasted_iota(jnp.int32, (n, n), 1)
    base = epoch_offset / ((s + t).astype(f32) + epoch_offset)
    return base + jnp.where(s == t, gain_row, 0.0)


def column(row):
    n = row.shape[-1]
    eye = lax.broadcasted_iota(jnp.int32, (n, n), 0) == lax.broadcasted_iota(jnp.int32, (n, n), 1)
    return jnp.sum(jnp.where(eye, row, 0.0), axis=1, keepdims=True)


def sides(features, length_scale, width):
    n, own = features.shape
    scaled = features * column(math.sqrt(math.log2(math.e)) / length_scale)
    hi = scaled.astype(bf16)
    lo = (scaled - hi.astype(f32)).astype(bf16)
    col = lax.broadcasted_iota(jnp.int32, (n, width), 1)
    row = lax.broadcasted_iota(jnp.int32, (n, width), 0)
    first, second, third = (col == row + k * n for k in range(3))
    lane = lax.broadcasted_iota(jnp.int32, (own, width), 1)

    def place(x, where):
        spot = jnp.where(where, 1.0, 0.0).astype(bf16)
        return lax.dot_general(x, spot, (((0,), (0,)), ((), ())), preferred_element_type=f32)

    left = place(hi, first | second) + place(lo, third)
    right = place(hi, first | third) + place(lo, second)
    sq = -0.5 * jnp.sum(left * right, axis=1, keepdims=True)
    sq0 = sq.astype(bf16).astype(f32)
    sq1 = (sq - sq0).astype(bf16).astype(f32)
    sq2 = sq - sq0 - sq1

    def tail(x, squares, ones):
        for k, piece in enumerate((sq0, sq1, sq2)):
            x = jnp.where(lane == squares + k, piece, x)
        return jnp.where((lane >= ones) & (lane < ones + 3), 1.0, x).astype(bf16)

    return tail(left, 3 * n, 3 * n + 3), tail(right, 3 * n + 3, 3 * n)


def seen(lengths, own, width):
    lane = lax.broadcasted_iota(jnp.int32, (own, width), 1).astype(f32)
    return (lane < column(lengths.astype(f32))).astype(f32)


def prepare(observed, lengths, features, length_scale, epoch_gain):
    own, width = observed.shape

    def body(obs_ref, len_ref, feat_ref, scale_ref, gain_ref, v_ref, mask_ref, ek_ref, out_ref, left_ref):
        left, right = sides(feat_ref[...], scale_ref[...], width)
        left_ref[...] = left
        lane = lax.broadcasted_iota(jnp.int32, (own, width), 1).astype(f32)
        mask = (lane < column(len_ref[...].astype(f32))).astype(f32)
        v = mask * obs_ref[...]
        ek = epoch_matrix(gain_ref[...])
        mask_ref[...] = mask
        v_ref[...] = v
        ek_ref[...] = ek
        w = jnp.dot(v, ek, precision=HIGHEST, preferred_element_type=f32)
        out_ref[:own, :] = w.astype(bf16)
        out_ref[own:, :] = right

    return pl.pallas_call(
        body,
        out_shape=(
            jax.ShapeDtypeStruct((own, width), f32),
            jax.ShapeDtypeStruct((own, width), f32),
            jax.ShapeDtypeStruct((width, width), f32),
            jax.ShapeDtypeStruct((2 * own, width), bf16),
            jax.ShapeDtypeStruct((own, width), bf16),
        ),
        in_specs=[VMEM] * 5,
        out_specs=(VMEM,) * 5,
        name="prepare",
    )(observed, lengths, features, length_scale, epoch_gain)


def across(x):
    ones = jnp.ones((x.shape[1], x.shape[1]), f32)
    return jnp.dot(x, ones, precision=HIGHEST, preferred_element_type=f32)


def pick(n, width):
    return jnp.arange(width)[None, :] == jnp.arange(n)[:, None]


def measure(v0, v1, v2):
    m = [jnp.sum(a * b, axis=0) for a, b in ((v0, v0), (v0, v1), (v1, v1), (v1, v2))]
    m = across(jnp.stack(m))
    return jnp.sum(jnp.where(pick(*m.shape), m, 0.0), axis=0, keepdims=True)


def finish(moments, v0, v1, v2):
    m = jnp.sum(moments, axis=0, keepdims=True)
    m = across(jnp.where(pick(4, m.shape[1]), m, 0.0))
    m0, m1, m2, m3 = (m[k : k + 1] for k in range(4))
    alpha = m0 / m1
    norm = m0 + alpha * (alpha * m2 - 2.0 * m1)
    keep = 1.0 + norm / m0
    curve = keep * (keep * m1 - 2.0 * alpha * m2) + alpha * alpha * m3
    again = norm / curve
    on0 = alpha + again * keep
    on1 = again * alpha
    return on0 * v0 - on1 * v1, v0 - on0 * v1 + on1 * v2


def block_kernel(left, right):
    e = lax.dot_general(left, right, (((1,), (1,)), ((), ())), preferred_element_type=f32)
    return jnp.exp2(jnp.minimum(e, 0.0)).astype(bf16)


def per_device(observed, lengths, features, length_scale, epoch_gain):
    own, width = observed.shape
    features, length_scale = features.T, length_scale[None, :]
    lengths, epoch_gain = lengths[None, :], epoch_gain[None, :]
    v0, mask, ek, outgoing, left = prepare(observed, lengths, features, length_scale, epoch_gain)
    here = to_all(outgoing, Z)
    line = around(left, X, jnp.zeros((lax.axis_size(X) * own, width), bf16))
    lefts = around(line, Y, jnp.zeros((lax.axis_size(Y) * line.shape[0], width), bf16))
    there = ahead(here, C, 1)
    k_here = block_kernel(lefts, here[:, own:].reshape(-1, width))
    k_there = block_kernel(lefts, there[:, own:].reshape(-1, width))

    def product(w_here, w_there):
        part = jnp.dot(k_here, w_here, preferred_element_type=f32)
        part = part + jnp.dot(k_there, w_there, preferred_element_type=f32)
        top = jnp.maximum(*(jnp.max(jnp.abs(w.astype(f32)), axis=0) for w in (w_here, w_there)))
        power = jnp.ceil(jnp.log2(jnp.maximum(top, 1e-30) * (2 * w_here.shape[0])))
        part = (part * jnp.exp2(15.0 - power)).astype(f16).reshape(-1, own, width)
        tail = jnp.broadcast_to(power.astype(f16), (part.shape[0], 8, width))
        got = lax.all_to_all(
            jnp.concatenate([part, tail], axis=1), (Y, X), split_axis=0, concat_axis=0, tiled=True
        )
        scale = jnp.exp2(got[:, own : own + 1].astype(f32) - 15.0)
        return jnp.sum(got[:, :own].astype(f32) * scale, axis=0)

    p = product(here[:, :own].reshape(-1, width), there[:, :own].reshape(-1, width))
    v1 = mask * p + noise_level * v0
    w = jnp.dot(mask * v1, ek, precision=HIGHEST, preferred_element_type=f32).astype(bf16)
    w_here = to_all(w, Z).reshape(-1, width)
    p = product(w_here, ahead(w_here, C, 1))
    v2 = mask * p + noise_level * v1
    m = measure(v0, v1, v2)
    m = to_all(m + ahead(m, C, 1), (Y, Z, X)).reshape(-1, width)
    return finish(m, v0, v1, v2)


def solution(mesh):
    torus = Mesh(mesh.devices.reshape(4, 2, 8, 4), ALL)
    in_specs = (P(ALL, None), P(ALL), P(ALL, None), P(), P())
    out_specs = (P(ALL, None), P(ALL, None))
    return jax.shard_map(
        per_device, mesh=torus, in_specs=in_specs, out_specs=out_specs, check_vma=False
    )
```

```python
import math

import jax
import jax.numpy as jnp
from jax import lax
from jax.experimental import pallas as pl
from jax.experimental.pallas import tpu as pltpu
from jax.sharding import Mesh
from jax.sharding import PartitionSpec as P

Y, C, Z, X = "y", "c", "z", "x"
ALL = (Y, C, Z, X)

noise_level = 0.3
epoch_offset = 16.0
bf16 = jnp.bfloat16
f32 = jnp.float32
f16 = jnp.float16
HIGHEST = lax.Precision.HIGHEST
VMEM = pl.BlockSpec(memory_space=pltpu.VMEM)
ANY = pl.BlockSpec(memory_space=pl.ANY)


def ahead(x, axis, k):
    n = lax.axis_size(axis)
    return lax.ppermute(x, axis, [((i + k) % n, i) for i in range(n)])


def shifted(x, axis):
    return [ahead(x, axis, k) for k in range(1, lax.axis_size(axis))]


def in_order(x, others, axis, base):
    n, me = lax.axis_size(axis), lax.axis_index(axis)
    for k, block in enumerate([x, *others]):
        base = lax.dynamic_update_slice_in_dim(base, block, (me + k) % n * x.shape[0], 0)
    return base


def to_all(x, axes):
    copies = jnp.broadcast_to(x, (lax.axis_size(axes), *x.shape))
    return lax.all_to_all(copies, axes, split_axis=0, concat_axis=0, tiled=True)


def epoch_matrix(gain_row):
    n = gain_row.shape[-1]
    s = lax.broadcasted_iota(jnp.int32, (n, n), 0)
    t = lax.broadcasted_iota(jnp.int32, (n, n), 1)
    base = epoch_offset / ((s + t).astype(f32) + epoch_offset)
    return base + jnp.where(s == t, gain_row, 0.0)


def column(row):
    n = row.shape[-1]
    eye = lax.broadcasted_iota(jnp.int32, (n, n), 0) == lax.broadcasted_iota(jnp.int32, (n, n), 1)
    return jnp.sum(jnp.where(eye, row, 0.0), axis=1, keepdims=True)


def sides(features, length_scale, width):
    n, own = features.shape
    scaled = features * column(math.sqrt(math.log2(math.e)) / length_scale)
    hi = scaled.astype(bf16)
    lo = (scaled - hi.astype(f32)).astype(bf16)
    col = lax.broadcasted_iota(jnp.int32, (n, width), 1)
    row = lax.broadcasted_iota(jnp.int32, (n, width), 0)
    first, second, third = (col == row + k * n for k in range(3))
    lane = lax.broadcasted_iota(jnp.int32, (own, width), 1)

    def place(x, where):
        spot = jnp.where(where, 1.0, 0.0).astype(bf16)
        return lax.dot_general(x, spot, (((0,), (0,)), ((), ())), preferred_element_type=f32)

    left = place(hi, first | second) + place(lo, third)
    right = place(hi, first | third) + place(lo, second)
    sq = -0.5 * jnp.sum(left * right, axis=1, keepdims=True)
    sq0 = sq.astype(bf16).astype(f32)
    sq1 = (sq - sq0).astype(bf16).astype(f32)
    sq2 = sq - sq0 - sq1

    def tail(x, squares, ones):
        for k, piece in enumerate((sq0, sq1, sq2)):
            x = jnp.where(lane == squares + k, piece, x)
        return jnp.where((lane >= ones) & (lane < ones + 3), 1.0, x).astype(bf16)

    return tail(left, 3 * n, 3 * n + 3), tail(right, 3 * n + 3, 3 * n)


def seen(lengths, own, width):
    lane = lax.broadcasted_iota(jnp.int32, (own, width), 1).astype(f32)
    return (lane < column(lengths.astype(f32))).astype(f32)


def prepare(observed, lengths, features, length_scale, epoch_gain, copies):
    own, width = observed.shape

    def body(obs_ref, len_ref, feat_ref, scale_ref, gain_ref, v_ref, mask_ref, ek_ref, out_ref, left_ref):
        left, right = sides(feat_ref[...], scale_ref[...], width)
        left_ref[...] = left
        lane = lax.broadcasted_iota(jnp.int32, (own, width), 1).astype(f32)
        mask = (lane < column(len_ref[...].astype(f32))).astype(f32)
        v = mask * obs_ref[...]
        ek = epoch_matrix(gain_ref[...])
        mask_ref[...] = mask
        v_ref[...] = v
        ek_ref[...] = ek
        w = jnp.dot(v, ek, precision=HIGHEST, preferred_element_type=f32)
        w = w.astype(bf16)
        for k in range(copies):
            out_ref[k, :own, :] = w
            out_ref[k, own:, :] = right

    return pl.pallas_call(
        body,
        out_shape=(
            jax.ShapeDtypeStruct((own, width), f32),
            jax.ShapeDtypeStruct((own, width), f32),
            jax.ShapeDtypeStruct((width, width), f32),
            jax.ShapeDtypeStruct((copies, 2 * own, width), bf16),
            jax.ShapeDtypeStruct((own, width), bf16),
        ),
        in_specs=[VMEM] * 5,
        out_specs=(VMEM,) * 5,
        name="prepare",
    )(observed, lengths, features, length_scale, epoch_gain)


def across(x):
    ones = jnp.ones((x.shape[1], x.shape[1]), f32)
    return jnp.dot(x, ones, precision=HIGHEST, preferred_element_type=f32)


def pick(n, width):
    return jnp.arange(width)[None, :] == jnp.arange(n)[:, None]


def measure(v0, v1, v2):
    m = [jnp.sum(a * b, axis=0) for a, b in ((v0, v0), (v0, v1), (v1, v1), (v1, v2))]
    m = across(jnp.stack(m))
    return jnp.sum(jnp.where(pick(*m.shape), m, 0.0), axis=0, keepdims=True)


def finish(moments, v0, v1, v2):
    m = jnp.sum(moments, axis=0, keepdims=True)
    m = across(jnp.where(pick(4, m.shape[1]), m, 0.0))
    m0, m1, m2, m3 = (m[k : k + 1] for k in range(4))
    alpha = m0 / m1
    norm = m0 + alpha * (alpha * m2 - 2.0 * m1)
    keep = 1.0 + norm / m0
    curve = keep * (keep * m1 - 2.0 * alpha * m2) + alpha * alpha * m3
    again = norm / curve
    on0 = alpha + again * keep
    on1 = again * alpha
    return on0 * v0 - on1 * v1, v0 - on0 * v1 + on1 * v2


def block_kernel(left, right):
    e = lax.dot_general(left, right, (((1,), (1,)), ((), ())), preferred_element_type=f32)
    return jnp.exp2(jnp.minimum(e, 0.0)).astype(bf16)


def per_device(observed, lengths, features, length_scale, epoch_gain):
    own, width = observed.shape
    features, length_scale = features.T, length_scale[None, :]
    lengths, epoch_gain = lengths[None, :], epoch_gain[None, :]
    v0, mask, ek, outgoing, left = prepare(
        observed, lengths, features, length_scale, epoch_gain, lax.axis_size(Z)
    )
    others = shifted(left, X)
    outgoing, others = lax.optimization_barrier((outgoing, others))
    here = lax.all_to_all(outgoing, Z, split_axis=0, concat_axis=0, tiled=True)
    there = ahead(here, C, 1)
    line = in_order(left, others, X, jnp.zeros((lax.axis_size(X) * own, width), bf16))
    lefts = in_order(line, shifted(line, Y), Y, here.reshape(-1, width))
    k_here = block_kernel(lefts, here[:, own:].reshape(-1, width))
    k_there = block_kernel(lefts, there[:, own:].reshape(-1, width))

    def product(w_here, w_there):
        part = jnp.dot(k_here, w_here, preferred_element_type=f32)
        part = part + jnp.dot(k_there, w_there, preferred_element_type=f32)
        top = jnp.maximum(*(jnp.max(jnp.abs(w.astype(f32)), axis=0) for w in (w_here, w_there)))
        power = jnp.ceil(jnp.log2(jnp.maximum(top, 1e-30) * (2 * w_here.shape[0])))
        part = (part * jnp.exp2(15.0 - power)).astype(f16).reshape(-1, own, width)
        tail = jnp.broadcast_to(power.astype(f16), (part.shape[0], 8, width))
        got = lax.all_to_all(
            jnp.concatenate([part, tail], axis=1), (Y, X), split_axis=0, concat_axis=0, tiled=True
        )
        scale = jnp.exp2(got[:, own : own + 1].astype(f32) - 15.0)
        return jnp.sum(got[:, :own].astype(f32) * scale, axis=0)

    p = product(here[:, :own].reshape(-1, width), there[:, :own].reshape(-1, width))
    v1 = mask * p + noise_level * v0
    w = jnp.dot(mask * v1, ek, precision=HIGHEST, preferred_element_type=f32).astype(bf16)
    w_here = to_all(w, Z).reshape(-1, width)
    p = product(w_here, ahead(w_here, C, 1))
    v2 = mask * p + noise_level * v1
    m = measure(v0, v1, v2)
    m = to_all(m + ahead(m, C, 1), (Y, Z, X)).reshape(-1, width)
    return finish(m, v0, v1, v2)


def solution(mesh):
    torus = Mesh(mesh.devices.reshape(4, 2, 8, 4), ALL)
    in_specs = (P(ALL, None), P(ALL), P(ALL, None), P(), P())
    out_specs = (P(ALL, None), P(ALL, None))
    return jax.shard_map(
        per_device, mesh=torus, in_specs=in_specs, out_specs=out_specs, check_vma=False
    )
```

```python
import math

import jax
import jax.numpy as jnp
from jax import lax
from jax.experimental import pallas as pl
from jax.experimental.pallas import tpu as pltpu
from jax.sharding import Mesh
from jax.sharding import PartitionSpec as P

Y, C, Z, X = "y", "c", "z", "x"
ALL = (Y, C, Z, X)

noise_level = 0.3
epoch_offset = 16.0
bf16 = jnp.bfloat16
f32 = jnp.float32
f16 = jnp.float16
HIGHEST = lax.Precision.HIGHEST
VMEM = pl.BlockSpec(memory_space=pltpu.VMEM)
ANY = pl.BlockSpec(memory_space=pl.ANY)


def ahead(x, axis, k):
    n = lax.axis_size(axis)
    return lax.ppermute(x, axis, [((i + k) % n, i) for i in range(n)])


def around(x, axis, base):
    n, me = lax.axis_size(axis), lax.axis_index(axis)
    for k in range(n):
        block = ahead(x, axis, k) if k else x
        base = lax.dynamic_update_slice_in_dim(base, block, (me + k) % n * x.shape[0], 0)
    return base


def to_all(x, axes):
    copies = jnp.broadcast_to(x, (lax.axis_size(axes), *x.shape))
    return lax.all_to_all(copies, axes, split_axis=0, concat_axis=0, tiled=True)


def epoch_matrix(gain_row):
    n = gain_row.shape[-1]
    s = lax.broadcasted_iota(jnp.int32, (n, n), 0)
    t = lax.broadcasted_iota(jnp.int32, (n, n), 1)
    base = epoch_offset / ((s + t).astype(f32) + epoch_offset)
    return base + jnp.where(s == t, gain_row, 0.0)


def column(row):
    n = row.shape[-1]
    eye = lax.broadcasted_iota(jnp.int32, (n, n), 0) == lax.broadcasted_iota(jnp.int32, (n, n), 1)
    return jnp.sum(jnp.where(eye, row, 0.0), axis=1, keepdims=True)


def sides(features, length_scale, width):
    n, own = features.shape
    scaled = features * column(math.sqrt(math.log2(math.e)) / length_scale)
    hi = scaled.astype(bf16)
    lo = (scaled - hi.astype(f32)).astype(bf16)
    col = lax.broadcasted_iota(jnp.int32, (n, width), 1)
    row = lax.broadcasted_iota(jnp.int32, (n, width), 0)
    first, second, third = (col == row + k * n for k in range(3))
    lane = lax.broadcasted_iota(jnp.int32, (own, width), 1)

    def place(x, where):
        spot = jnp.where(where, 1.0, 0.0).astype(bf16)
        return lax.dot_general(x, spot, (((0,), (0,)), ((), ())), preferred_element_type=f32)

    left = place(hi, first | second) + place(lo, third)
    right = place(hi, first | third) + place(lo, second)
    sq = -0.5 * jnp.sum(left * right, axis=1, keepdims=True)
    sq0 = sq.astype(bf16).astype(f32)
    sq1 = (sq - sq0).astype(bf16).astype(f32)
    sq2 = sq - sq0 - sq1

    def tail(x, squares, ones):
        for k, piece in enumerate((sq0, sq1, sq2)):
            x = jnp.where(lane == squares + k, piece, x)
        return jnp.where((lane >= ones) & (lane < ones + 3), 1.0, x).astype(bf16)

    return tail(left, 3 * n, 3 * n + 3), tail(right, 3 * n + 3, 3 * n)


def seen(lengths, own, width):
    lane = lax.broadcasted_iota(jnp.int32, (own, width), 1).astype(f32)
    return (lane < column(lengths.astype(f32))).astype(f32)


def prepare(observed, lengths, features, length_scale, epoch_gain, copies):
    own, width = observed.shape

    def body(obs_ref, len_ref, feat_ref, scale_ref, gain_ref, v_ref, mask_ref, ek_ref, out_ref, left_ref):
        left, right = sides(feat_ref[...], scale_ref[...], width)
        left_ref[...] = left
        lane = lax.broadcasted_iota(jnp.int32, (own, width), 1).astype(f32)
        mask = (lane < column(len_ref[...].astype(f32))).astype(f32)
        v = mask * obs_ref[...]
        ek = epoch_matrix(gain_ref[...])
        mask_ref[...] = mask
        v_ref[...] = v
        ek_ref[...] = ek
        w = jnp.dot(v, ek, precision=HIGHEST, preferred_element_type=f32)
        w = w.astype(bf16)
        for k in range(copies):
            out_ref[k, :own, :] = w
            out_ref[k, own:, :] = right

    return pl.pallas_call(
        body,
        out_shape=(
            jax.ShapeDtypeStruct((own, width), f32),
            jax.ShapeDtypeStruct((own, width), f32),
            jax.ShapeDtypeStruct((width, width), f32),
            jax.ShapeDtypeStruct((copies, 2 * own, width), bf16),
            jax.ShapeDtypeStruct((own, width), bf16),
        ),
        in_specs=[VMEM] * 5,
        out_specs=(VMEM,) * 5,
        name="prepare",
    )(observed, lengths, features, length_scale, epoch_gain)


def across(x):
    ones = jnp.ones((x.shape[1], x.shape[1]), f32)
    return jnp.dot(x, ones, precision=HIGHEST, preferred_element_type=f32)


def pick(n, width):
    return jnp.arange(width)[None, :] == jnp.arange(n)[:, None]


def measure(v0, v1, v2):
    m = [jnp.sum(a * b, axis=0) for a, b in ((v0, v0), (v0, v1), (v1, v1), (v1, v2))]
    m = across(jnp.stack(m))
    return jnp.sum(jnp.where(pick(*m.shape), m, 0.0), axis=0, keepdims=True)


def finish(moments, v0, v1, v2):
    m = jnp.sum(moments, axis=0, keepdims=True)
    m = across(jnp.where(pick(4, m.shape[1]), m, 0.0))
    m0, m1, m2, m3 = (m[k : k + 1] for k in range(4))
    alpha = m0 / m1
    norm = m0 + alpha * (alpha * m2 - 2.0 * m1)
    keep = 1.0 + norm / m0
    curve = keep * (keep * m1 - 2.0 * alpha * m2) + alpha * alpha * m3
    again = norm / curve
    on0 = alpha + again * keep
    on1 = again * alpha
    return on0 * v0 - on1 * v1, v0 - on0 * v1 + on1 * v2


def block_kernel(left, right):
    e = lax.dot_general(left, right, (((1,), (1,)), ((), ())), preferred_element_type=f32)
    return jnp.exp2(jnp.minimum(e, 0.0)).astype(bf16)


def per_device(observed, lengths, features, length_scale, epoch_gain):
    own, width = observed.shape
    features, length_scale = features.T, length_scale[None, :]
    lengths, epoch_gain = lengths[None, :], epoch_gain[None, :]
    v0, mask, ek, outgoing, left = prepare(
        observed, lengths, features, length_scale, epoch_gain, lax.axis_size(Z)
    )
    here = lax.all_to_all(outgoing, Z, split_axis=0, concat_axis=0, tiled=True)
    line = around(left, X, jnp.zeros((lax.axis_size(X) * own, width), bf16))
    lefts = around(line, Y, jnp.zeros((lax.axis_size(Y) * line.shape[0], width), bf16))
    there = ahead(here, C, 1)
    k_here = block_kernel(lefts, here[:, own:].reshape(-1, width))
    k_there = block_kernel(lefts, there[:, own:].reshape(-1, width))

    def product(w_here, w_there):
        part = jnp.dot(k_here, w_here, preferred_element_type=f32)
        part = part + jnp.dot(k_there, w_there, preferred_element_type=f32)
        top = jnp.maximum(*(jnp.max(jnp.abs(w.astype(f32)), axis=0) for w in (w_here, w_there)))
        power = jnp.ceil(jnp.log2(jnp.maximum(top, 1e-30) * (2 * w_here.shape[0])))
        part = (part * jnp.exp2(15.0 - power)).astype(f16).reshape(-1, own, width)
        tail = jnp.broadcast_to(power.astype(f16), (part.shape[0], 8, width))
        got = lax.all_to_all(
            jnp.concatenate([part, tail], axis=1), (Y, X), split_axis=0, concat_axis=0, tiled=True
        )
        scale = jnp.exp2(got[:, own : own + 1].astype(f32) - 15.0)
        return jnp.sum(got[:, :own].astype(f32) * scale, axis=0)

    p = product(here[:, :own].reshape(-1, width), there[:, :own].reshape(-1, width))
    v1 = mask * p + noise_level * v0
    w = jnp.dot(mask * v1, ek, precision=HIGHEST, preferred_element_type=f32).astype(bf16)
    w_here = to_all(w, Z).reshape(-1, width)
    p = product(w_here, ahead(w_here, C, 1))
    v2 = mask * p + noise_level * v1
    m = measure(v0, v1, v2)
    m = to_all(m + ahead(m, C, 1), (Y, Z, X)).reshape(-1, width)
    return finish(m, v0, v1, v2)


def solution(mesh):
    torus = Mesh(mesh.devices.reshape(4, 2, 8, 4), ALL)
    in_specs = (P(ALL, None), P(ALL), P(ALL, None), P(), P())
    out_specs = (P(ALL, None), P(ALL, None))
    return jax.shard_map(
        per_device, mesh=torus, in_specs=in_specs, out_specs=out_specs, check_vma=False
    )
```

```python
import math

import jax
import jax.numpy as jnp
from jax import lax
from jax.experimental import pallas as pl
from jax.experimental.pallas import tpu as pltpu
from jax.sharding import Mesh
from jax.sharding import PartitionSpec as P

Y, C, Z, X = "y", "c", "z", "x"
ALL = (Y, C, Z, X)

noise_level = 0.3
epoch_offset = 16.0
bf16 = jnp.bfloat16
f32 = jnp.float32
f16 = jnp.float16
HIGHEST = lax.Precision.HIGHEST
VMEM = pl.BlockSpec(memory_space=pltpu.VMEM)
ANY = pl.BlockSpec(memory_space=pl.ANY)


def ahead(x, axis, k):
    n = lax.axis_size(axis)
    return lax.ppermute(x, axis, [((i + k) % n, i) for i in range(n)])


def around(x, axis, base, behind=None):
    n, me = lax.axis_size(axis), lax.axis_index(axis)
    for k in range(n):
        block = ahead(x, axis, k) if k else x
        if k == 1 and behind is not None:
            block, behind = lax.optimization_barrier((block, behind))
        base = lax.dynamic_update_slice_in_dim(base, block, (me + k) % n * x.shape[0], 0)
    return base


def to_all(x, axes):
    copies = jnp.broadcast_to(x, (lax.axis_size(axes), *x.shape))
    return lax.all_to_all(copies, axes, split_axis=0, concat_axis=0, tiled=True)


def epoch_matrix(gain_row):
    n = gain_row.shape[-1]
    s = lax.broadcasted_iota(jnp.int32, (n, n), 0)
    t = lax.broadcasted_iota(jnp.int32, (n, n), 1)
    base = epoch_offset / ((s + t).astype(f32) + epoch_offset)
    return base + jnp.where(s == t, gain_row, 0.0)


def column(row):
    n = row.shape[-1]
    eye = lax.broadcasted_iota(jnp.int32, (n, n), 0) == lax.broadcasted_iota(jnp.int32, (n, n), 1)
    return jnp.sum(jnp.where(eye, row, 0.0), axis=1, keepdims=True)


def sides(features, length_scale, width):
    n, own = features.shape
    scaled = features * column(math.sqrt(math.log2(math.e)) / length_scale)
    hi = scaled.astype(bf16)
    lo = (scaled - hi.astype(f32)).astype(bf16)
    col = lax.broadcasted_iota(jnp.int32, (n, width), 1)
    row = lax.broadcasted_iota(jnp.int32, (n, width), 0)
    first, second, third = (col == row + k * n for k in range(3))
    lane = lax.broadcasted_iota(jnp.int32, (own, width), 1)

    def place(x, where):
        spot = jnp.where(where, 1.0, 0.0).astype(bf16)
        return lax.dot_general(x, spot, (((0,), (0,)), ((), ())), preferred_element_type=f32)

    left = place(hi, first | second) + place(lo, third)
    right = place(hi, first | third) + place(lo, second)
    sq = -0.5 * jnp.sum(left * right, axis=1, keepdims=True)
    sq0 = sq.astype(bf16).astype(f32)
    sq1 = (sq - sq0).astype(bf16).astype(f32)
    sq2 = sq - sq0 - sq1

    def tail(x, squares, ones):
        for k, piece in enumerate((sq0, sq1, sq2)):
            x = jnp.where(lane == squares + k, piece, x)
        return jnp.where((lane >= ones) & (lane < ones + 3), 1.0, x).astype(bf16)

    return tail(left, 3 * n, 3 * n + 3), tail(right, 3 * n + 3, 3 * n)


def seen(lengths, own, width):
    lane = lax.broadcasted_iota(jnp.int32, (own, width), 1).astype(f32)
    return (lane < column(lengths.astype(f32))).astype(f32)


def prepare(observed, lengths, features, length_scale, epoch_gain, copies):
    own, width = observed.shape

    def body(obs_ref, len_ref, feat_ref, scale_ref, gain_ref, v_ref, mask_ref, ek_ref, out_ref, left_ref):
        left, right = sides(feat_ref[...], scale_ref[...], width)
        left_ref[...] = left
        lane = lax.broadcasted_iota(jnp.int32, (own, width), 1).astype(f32)
        mask = (lane < column(len_ref[...].astype(f32))).astype(f32)
        v = mask * obs_ref[...]
        ek = epoch_matrix(gain_ref[...])
        mask_ref[...] = mask
        v_ref[...] = v
        ek_ref[...] = ek
        w = jnp.dot(v, ek, precision=HIGHEST, preferred_element_type=f32)
        w = w.astype(bf16)
        for k in range(copies):
            out_ref[k, :own, :] = w
            out_ref[k, own:, :] = right

    return pl.pallas_call(
        body,
        out_shape=(
            pltpu.VMEM((own, width), f32),
            pltpu.VMEM((own, width), f32),
            pltpu.VMEM((width, width), f32),
            jax.ShapeDtypeStruct((copies, 2 * own, width), bf16),
            pltpu.VMEM((own, width), bf16),
        ),
        in_specs=[VMEM] * 5,
        out_specs=(VMEM,) * 5,
        name="prepare",
    )(observed, lengths, features, length_scale, epoch_gain)


def across(x):
    ones = jnp.ones((x.shape[1], x.shape[1]), f32)
    return jnp.dot(x, ones, precision=HIGHEST, preferred_element_type=f32)


def pick(n, width):
    return jnp.arange(width)[None, :] == jnp.arange(n)[:, None]


def measure(v0, v1, v2):
    m = [jnp.sum(a * b, axis=0) for a, b in ((v0, v0), (v0, v1), (v1, v1), (v1, v2))]
    m = across(jnp.stack(m))
    return jnp.sum(jnp.where(pick(*m.shape), m, 0.0), axis=0, keepdims=True)


def finish(moments, v0, v1, v2):
    m = jnp.sum(moments, axis=0, keepdims=True)
    m = across(jnp.where(pick(4, m.shape[1]), m, 0.0))
    m0, m1, m2, m3 = (m[k : k + 1] for k in range(4))
    alpha = m0 / m1
    norm = m0 + alpha * (alpha * m2 - 2.0 * m1)
    keep = 1.0 + norm / m0
    curve = keep * (keep * m1 - 2.0 * alpha * m2) + alpha * alpha * m3
    again = norm / curve
    on0 = alpha + again * keep
    on1 = again * alpha
    return on0 * v0 - on1 * v1, v0 - on0 * v1 + on1 * v2


def block_kernel(left, right):
    e = lax.dot_general(left, right, (((1,), (1,)), ((), ())), preferred_element_type=f32)
    return jnp.exp2(jnp.minimum(e, 0.0)).astype(bf16)


def per_device(observed, lengths, features, length_scale, epoch_gain):
    own, width = observed.shape
    features, length_scale = features.T, length_scale[None, :]
    lengths, epoch_gain = lengths[None, :], epoch_gain[None, :]
    v0, mask, ek, outgoing, left = prepare(
        observed, lengths, features, length_scale, epoch_gain, lax.axis_size(Z)
    )
    here = lax.all_to_all(outgoing, Z, split_axis=0, concat_axis=0, tiled=True)
    there = ahead(here, C, 1)
    line = around(left, X, jnp.zeros((lax.axis_size(X) * own, width), bf16))
    lefts = around(line, Y, jnp.zeros((lax.axis_size(Y) * line.shape[0], width), bf16), there)
    k_here = block_kernel(lefts, here[:, own:].reshape(-1, width))
    k_there = block_kernel(lefts, there[:, own:].reshape(-1, width))

    def product(w_here, w_there):
        part = jnp.dot(k_here, w_here, preferred_element_type=f32)
        part = part + jnp.dot(k_there, w_there, preferred_element_type=f32)
        top = jnp.maximum(*(jnp.max(jnp.abs(w.astype(f32)), axis=0) for w in (w_here, w_there)))
        power = jnp.ceil(jnp.log2(jnp.maximum(top, 1e-30) * (2 * w_here.shape[0])))
        part = (part * jnp.exp2(15.0 - power)).astype(f16).reshape(-1, own, width)
        tail = jnp.broadcast_to(power.astype(f16), (part.shape[0], 8, width))
        got = lax.all_to_all(
            jnp.concatenate([part, tail], axis=1), (Y, X), split_axis=0, concat_axis=0, tiled=True
        )
        scale = jnp.exp2(got[:, own : own + 1].astype(f32) - 15.0)
        return jnp.sum(got[:, :own].astype(f32) * scale, axis=0)

    p = product(here[:, :own].reshape(-1, width), there[:, :own].reshape(-1, width))
    v1 = mask * p + noise_level * v0
    w = jnp.dot(mask * v1, ek, precision=HIGHEST, preferred_element_type=f32).astype(bf16)
    w_here = to_all(w, Z).reshape(-1, width)
    p = product(w_here, ahead(w_here, C, 1))
    v2 = mask * p + noise_level * v1
    m = measure(v0, v1, v2)
    m = to_all(m + ahead(m, C, 1), (Y, Z, X)).reshape(-1, width)
    return finish(m, v0, v1, v2)


def solution(mesh):
    torus = Mesh(mesh.devices.reshape(4, 2, 8, 4), ALL)
    in_specs = (P(ALL, None), P(ALL), P(ALL, None), P(), P())
    out_specs = (P(ALL, None), P(ALL, None))
    return jax.shard_map(
        per_device, mesh=torus, in_specs=in_specs, out_specs=out_specs, check_vma=False
    )
```

```python
import math

import jax
import jax.numpy as jnp
from jax import lax
from jax.experimental import pallas as pl
from jax.experimental.pallas import tpu as pltpu
from jax.sharding import Mesh
from jax.sharding import PartitionSpec as P

Y, C, Z, X = "y", "c", "z", "x"
ALL = (Y, C, Z, X)

noise_level = 0.3
epoch_offset = 16.0
bf16 = jnp.bfloat16
f32 = jnp.float32
f16 = jnp.float16
HIGHEST = lax.Precision.HIGHEST
VMEM = pl.BlockSpec(memory_space=pltpu.VMEM)
ANY = pl.BlockSpec(memory_space=pl.ANY)


def ahead(x, axis, k):
    n = lax.axis_size(axis)
    return lax.ppermute(x, axis, [((i + k) % n, i) for i in range(n)])


def around(x, axis, base, behind=None):
    n, me = lax.axis_size(axis), lax.axis_index(axis)
    for k in range(n):
        block = ahead(x, axis, k) if k else x
        if k == 1 and behind is not None:
            block, behind = lax.optimization_barrier((block, behind))
        base = lax.dynamic_update_slice_in_dim(base, block, (me + k) % n * x.shape[0], 0)
    return base


def to_all(x, axes):
    copies = jnp.broadcast_to(x, (lax.axis_size(axes), *x.shape))
    return lax.all_to_all(copies, axes, split_axis=0, concat_axis=0, tiled=True)


def epoch_matrix(gain_row):
    n = gain_row.shape[-1]
    s = lax.broadcasted_iota(jnp.int32, (n, n), 0)
    t = lax.broadcasted_iota(jnp.int32, (n, n), 1)
    base = epoch_offset / ((s + t).astype(f32) + epoch_offset)
    return base + jnp.where(s == t, gain_row, 0.0)


def column(row):
    n = row.shape[-1]
    eye = lax.broadcasted_iota(jnp.int32, (n, n), 0) == lax.broadcasted_iota(jnp.int32, (n, n), 1)
    return jnp.sum(jnp.where(eye, row, 0.0), axis=1, keepdims=True)


def sides(features, length_scale, width):
    n, own = features.shape
    scaled = features * column(math.sqrt(math.log2(math.e)) / length_scale)
    hi = scaled.astype(bf16)
    lo = (scaled - hi.astype(f32)).astype(bf16)
    col = lax.broadcasted_iota(jnp.int32, (n, width), 1)
    row = lax.broadcasted_iota(jnp.int32, (n, width), 0)
    first, second, third = (col == row + k * n for k in range(3))
    lane = lax.broadcasted_iota(jnp.int32, (own, width), 1)

    def place(x, where):
        spot = jnp.where(where, 1.0, 0.0).astype(bf16)
        return lax.dot_general(x, spot, (((0,), (0,)), ((), ())), preferred_element_type=f32)

    left = place(hi, first | second) + place(lo, third)
    right = place(hi, first | third) + place(lo, second)
    sq = -0.5 * jnp.sum(left * right, axis=1, keepdims=True)
    sq0 = sq.astype(bf16).astype(f32)
    sq1 = (sq - sq0).astype(bf16).astype(f32)
    sq2 = sq - sq0 - sq1

    def tail(x, squares, ones):
        for k, piece in enumerate((sq0, sq1, sq2)):
            x = jnp.where(lane == squares + k, piece, x)
        return jnp.where((lane >= ones) & (lane < ones + 3), 1.0, x).astype(bf16)

    return tail(left, 3 * n, 3 * n + 3), tail(right, 3 * n + 3, 3 * n)


def seen(lengths, own, width):
    lane = lax.broadcasted_iota(jnp.int32, (own, width), 1).astype(f32)
    return (lane < column(lengths.astype(f32))).astype(f32)


def prepare(observed, lengths, features, length_scale, epoch_gain, copies):
    own, width = observed.shape

    def body(obs_ref, len_ref, feat_ref, scale_ref, gain_ref, v_ref, mask_ref, ek_ref, out_ref, left_ref):
        left, right = sides(feat_ref[...], scale_ref[...], width)
        left_ref[...] = left
        lane = lax.broadcasted_iota(jnp.int32, (own, width), 1).astype(f32)
        mask = (lane < column(len_ref[...].astype(f32))).astype(f32)
        v = mask * obs_ref[...]
        ek = epoch_matrix(gain_ref[...])
        mask_ref[...] = mask
        v_ref[...] = v
        ek_ref[...] = ek
        w = jnp.dot(v, ek, precision=HIGHEST, preferred_element_type=f32)
        w = w.astype(bf16)
        for k in range(copies):
            out_ref[k, :own, :] = w
            out_ref[k, own:, :] = right

    return pl.pallas_call(
        body,
        out_shape=(
            pltpu.VMEM((own, width), f32),
            pltpu.VMEM((own, width), f32),
            pltpu.VMEM((width, width), f32),
            jax.ShapeDtypeStruct((copies, 2 * own, width), bf16),
            pltpu.VMEM((own, width), bf16),
        ),
        in_specs=[VMEM] * 5,
        out_specs=(VMEM,) * 5,
        name="prepare",
    )(observed, lengths, features, length_scale, epoch_gain)


def across(x):
    ones = jnp.ones((x.shape[1], x.shape[1]), f32)
    return jnp.dot(x, ones, precision=HIGHEST, preferred_element_type=f32)


def pick(n, width):
    return jnp.arange(width)[None, :] == jnp.arange(n)[:, None]


def measure(v0, v1, v2):
    m = [jnp.sum(a * b, axis=0) for a, b in ((v0, v0), (v0, v1), (v1, v1), (v1, v2))]
    m = across(jnp.stack(m))
    return jnp.sum(jnp.where(pick(*m.shape), m, 0.0), axis=0, keepdims=True)


def finish(moments, v0, v1, v2):
    m = jnp.sum(moments, axis=0, keepdims=True)
    m = across(jnp.where(pick(4, m.shape[1]), m, 0.0))
    m0, m1, m2, m3 = (m[k : k + 1] for k in range(4))
    t1, t2, t3 = m1 / m0, m2 / m1, m3 / m2
    alpha = (t2 - t1) / (t2 * (t3 - t2))
    on0 = (1.0 + alpha * t2) / t1
    on1 = alpha / t1
    return on0 * v0 - on1 * v1, v0 - on0 * v1 + on1 * v2


def block_kernel(left, right):
    e = lax.dot_general(left, right, (((1,), (1,)), ((), ())), preferred_element_type=f32)
    return jnp.exp2(jnp.minimum(e, 0.0)).astype(bf16)


def per_device(observed, lengths, features, length_scale, epoch_gain):
    own, width = observed.shape
    features, length_scale = features.T, length_scale[None, :]
    lengths, epoch_gain = lengths[None, :], epoch_gain[None, :]
    v0, mask, ek, outgoing, left = prepare(
        observed, lengths, features, length_scale, epoch_gain, lax.axis_size(Z)
    )
    here = lax.all_to_all(outgoing, Z, split_axis=0, concat_axis=0, tiled=True)
    there = ahead(here, C, 1)
    line = around(left, X, jnp.zeros((lax.axis_size(X) * own, width), bf16))
    lefts = around(line, Y, jnp.zeros((lax.axis_size(Y) * line.shape[0], width), bf16), there)
    k_all = block_kernel(lefts, jnp.concatenate([here[:, own:], there[:, own:]]).reshape(-1, width))
    k_here, k_there = k_all[:, : k_all.shape[1] // 2], k_all[:, k_all.shape[1] // 2 :]

    def product(w_here, w_there):
        part = jnp.dot(k_here, w_here, preferred_element_type=f32)
        part = part + jnp.dot(k_there, w_there, preferred_element_type=f32)
        top = jnp.maximum(*(jnp.max(jnp.abs(w.astype(f32)), axis=0) for w in (w_here, w_there)))
        power = jnp.ceil(jnp.log2(jnp.maximum(top, 1e-30) * (2 * w_here.shape[0])))
        part = (part * jnp.exp2(15.0 - power)).astype(f16).reshape(-1, own, width)
        tail = jnp.broadcast_to(power.astype(f16), (part.shape[0], 8, width))
        got = lax.all_to_all(
            jnp.concatenate([part, tail], axis=1), (Y, X), split_axis=0, concat_axis=0, tiled=True
        )
        scale = jnp.exp2(got[:, own : own + 1].astype(f32) - 15.0)
        return jnp.sum(got[:, :own].astype(f32) * scale, axis=0)

    p = product(here[:, :own].reshape(-1, width), there[:, :own].reshape(-1, width))
    v1 = mask * p + noise_level * v0
    w = jnp.dot(mask * v1, ek, precision=HIGHEST, preferred_element_type=f32).astype(bf16)
    w_here = to_all(w, Z).reshape(-1, width)
    p = product(w_here, ahead(w_here, C, 1))
    v2 = mask * p + noise_level * v1
    m = measure(v0, v1, v2)
    m = to_all(m + ahead(m, C, 1), (Y, Z, X)).reshape(-1, width)
    return finish(m, v0, v1, v2)


def solution(mesh):
    torus = Mesh(mesh.devices.reshape(4, 2, 8, 4), ALL)
    in_specs = (P(ALL, None), P(ALL), P(ALL, None), P(), P())
    out_specs = (P(ALL, None), P(ALL, None))
    return jax.shard_map(
        per_device, mesh=torus, in_specs=in_specs, out_specs=out_specs, check_vma=False
    )
```

```python
import math

import jax
import jax.numpy as jnp
from jax import lax
from jax.experimental import pallas as pl
from jax.experimental.pallas import tpu as pltpu
from jax.sharding import Mesh
from jax.sharding import PartitionSpec as P

Y, C, Z, X = "y", "c", "z", "x"
ALL = (Y, C, Z, X)

noise_level = 0.3
epoch_offset = 16.0
bf16 = jnp.bfloat16
f32 = jnp.float32
f16 = jnp.float16
HIGHEST = lax.Precision.HIGHEST
VMEM = pl.BlockSpec(memory_space=pltpu.VMEM)
ANY = pl.BlockSpec(memory_space=pl.ANY)


def ahead(x, axis, k):
    n = lax.axis_size(axis)
    return lax.ppermute(x, axis, [((i + k) % n, i) for i in range(n)])


def around(x, axis, base, behind=None):
    n, me = lax.axis_size(axis), lax.axis_index(axis)
    for k in range(n):
        block = ahead(x, axis, k) if k else x
        if k == n - 1 and behind is not None:
            block, behind = lax.optimization_barrier((block, behind))
        base = lax.dynamic_update_slice_in_dim(base, block, (me + k) % n * x.shape[0], 0)
    return base


def to_all(x, axes):
    copies = jnp.broadcast_to(x, (lax.axis_size(axes), *x.shape))
    return lax.all_to_all(copies, axes, split_axis=0, concat_axis=0, tiled=True)


def epoch_matrix(gain_row):
    n = gain_row.shape[-1]
    s = lax.broadcasted_iota(jnp.int32, (n, n), 0)
    t = lax.broadcasted_iota(jnp.int32, (n, n), 1)
    base = epoch_offset / ((s + t).astype(f32) + epoch_offset)
    return base + jnp.where(s == t, gain_row, 0.0)


def column(row):
    n = row.shape[-1]
    eye = lax.broadcasted_iota(jnp.int32, (n, n), 0) == lax.broadcasted_iota(jnp.int32, (n, n), 1)
    return jnp.sum(jnp.where(eye, row, 0.0), axis=1, keepdims=True)


def sides(features, length_scale, width):
    n, own = features.shape
    scaled = features * column(math.sqrt(math.log2(math.e)) / length_scale)
    hi = scaled.astype(bf16)
    lo = (scaled - hi.astype(f32)).astype(bf16)
    col = lax.broadcasted_iota(jnp.int32, (n, width), 1)
    row = lax.broadcasted_iota(jnp.int32, (n, width), 0)
    first, second, third = (col == row + k * n for k in range(3))
    lane = lax.broadcasted_iota(jnp.int32, (own, width), 1)

    def place(x, where):
        spot = jnp.where(where, 1.0, 0.0).astype(bf16)
        return lax.dot_general(x, spot, (((0,), (0,)), ((), ())), preferred_element_type=f32)

    left = place(hi, first | second) + place(lo, third)
    right = place(hi, first | third) + place(lo, second)
    sq = -0.5 * jnp.sum(left * right, axis=1, keepdims=True)
    sq0 = sq.astype(bf16).astype(f32)
    sq1 = (sq - sq0).astype(bf16).astype(f32)
    sq2 = sq - sq0 - sq1

    def tail(x, squares, ones):
        for k, piece in enumerate((sq0, sq1, sq2)):
            x = jnp.where(lane == squares + k, piece, x)
        return jnp.where((lane >= ones) & (lane < ones + 3), 1.0, x).astype(bf16)

    return tail(left, 3 * n, 3 * n + 3), tail(right, 3 * n + 3, 3 * n)


def seen(lengths, own, width):
    lane = lax.broadcasted_iota(jnp.int32, (own, width), 1).astype(f32)
    return (lane < column(lengths.astype(f32))).astype(f32)


def prepare(observed, lengths, features, length_scale, epoch_gain, copies):
    own, width = observed.shape

    def body(obs_ref, len_ref, feat_ref, scale_ref, gain_ref, v_ref, mask_ref, ek_ref, out_ref, left_ref):
        left, right = sides(feat_ref[...], scale_ref[...], width)
        left_ref[...] = left
        lane = lax.broadcasted_iota(jnp.int32, (own, width), 1).astype(f32)
        mask = (lane < column(len_ref[...].astype(f32))).astype(f32)
        v = mask * obs_ref[...]
        ek = epoch_matrix(gain_ref[...])
        mask_ref[...] = mask
        v_ref[...] = v
        ek_ref[...] = ek
        w = jnp.dot(v, ek, precision=HIGHEST, preferred_element_type=f32)
        w = w.astype(bf16)
        for k in range(copies):
            out_ref[k, :own, :] = w
            out_ref[k, own:, :] = right

    return pl.pallas_call(
        body,
        out_shape=(
            pltpu.VMEM((own, width), f32),
            pltpu.VMEM((own, width), f32),
            pltpu.VMEM((width, width), f32),
            jax.ShapeDtypeStruct((copies, 2 * own, width), bf16),
            pltpu.VMEM((own, width), bf16),
        ),
        in_specs=[VMEM] * 5,
        out_specs=(VMEM,) * 5,
        name="prepare",
    )(observed, lengths, features, length_scale, epoch_gain)


def across(x):
    ones = jnp.ones((x.shape[1], x.shape[1]), f32)
    return jnp.dot(x, ones, precision=HIGHEST, preferred_element_type=f32)


def pick(n, width):
    return jnp.arange(width)[None, :] == jnp.arange(n)[:, None]


def measure(v0, v1, v2):
    m = [jnp.sum(a * b, axis=0) for a, b in ((v0, v0), (v0, v1), (v1, v1), (v1, v2))]
    m = across(jnp.stack(m))
    return jnp.sum(jnp.where(pick(*m.shape), m, 0.0), axis=0, keepdims=True)


def finish(moments, v0, v1, v2):
    m = jnp.sum(moments, axis=0, keepdims=True)
    m = across(jnp.where(pick(4, m.shape[1]), m, 0.0))
    m0, m1, m2, m3 = (m[k : k + 1] for k in range(4))
    alpha = m0 / m1
    norm = m0 + alpha * (alpha * m2 - 2.0 * m1)
    keep = 1.0 + norm / m0
    curve = keep * (keep * m1 - 2.0 * alpha * m2) + alpha * alpha * m3
    again = norm / curve
    on0 = alpha + again * keep
    on1 = again * alpha
    return on0 * v0 - on1 * v1, v0 - on0 * v1 + on1 * v2


def block_kernel(left, right):
    e = lax.dot_general(left, right, (((1,), (1,)), ((), ())), preferred_element_type=f32)
    return jnp.exp2(jnp.minimum(e, 0.0)).astype(bf16)


def per_device(observed, lengths, features, length_scale, epoch_gain):
    own, width = observed.shape
    features, length_scale = features.T, length_scale[None, :]
    lengths, epoch_gain = lengths[None, :], epoch_gain[None, :]
    v0, mask, ek, outgoing, left = prepare(
        observed, lengths, features, length_scale, epoch_gain, lax.axis_size(Z)
    )
    here = lax.all_to_all(outgoing, Z, split_axis=0, concat_axis=0, tiled=True)
    there = ahead(here, C, 1)
    line = around(left, X, jnp.zeros((lax.axis_size(X) * own, width), bf16))
    lefts = around(line, Y, jnp.zeros((lax.axis_size(Y) * line.shape[0], width), bf16), there)
    k_here = block_kernel(lefts, here[:, own:].reshape(-1, width))
    k_there = block_kernel(lefts, there[:, own:].reshape(-1, width))

    def product(w_here, w_there):
        part = jnp.dot(k_here, w_here, preferred_element_type=f32)
        part = part + jnp.dot(k_there, w_there, preferred_element_type=f32)
        top = jnp.maximum(*(jnp.max(jnp.abs(w.astype(f32)), axis=0) for w in (w_here, w_there)))
        power = jnp.ceil(jnp.log2(jnp.maximum(top, 1e-30) * (2 * w_here.shape[0])))
        part = (part * jnp.exp2(15.0 - power)).astype(f16).reshape(-1, own, width)
        tail = jnp.broadcast_to(power.astype(f16), (part.shape[0], 8, width))
        got = lax.all_to_all(
            jnp.concatenate([part, tail], axis=1), (Y, X), split_axis=0, concat_axis=0, tiled=True
        )
        scale = jnp.exp2(got[:, own : own + 1].astype(f32) - 15.0)
        return jnp.sum(got[:, :own].astype(f32) * scale, axis=0)

    p = product(here[:, :own].reshape(-1, width), there[:, :own].reshape(-1, width))
    v1 = mask * p + noise_level * v0
    w = jnp.dot(mask * v1, ek, precision=HIGHEST, preferred_element_type=f32).astype(bf16)
    w_here = to_all(w, Z).reshape(-1, width)
    p = product(w_here, ahead(w_here, C, 1))
    v2 = mask * p + noise_level * v1
    m = measure(v0, v1, v2)
    m = to_all(m + ahead(m, C, 1), (Y, Z, X)).reshape(-1, width)
    return finish(m, v0, v1, v2)


def solution(mesh):
    torus = Mesh(mesh.devices.reshape(4, 2, 8, 4), ALL)
    in_specs = (P(ALL, None), P(ALL), P(ALL, None), P(), P())
    out_specs = (P(ALL, None), P(ALL, None))
    return jax.shard_map(
        per_device, mesh=torus, in_specs=in_specs, out_specs=out_specs, check_vma=False
    )
```
